32 devices in a mesh: wide: 8 (over y, x, core), narrow: 4 (over z).
Axes of the slice: x: 2, y: 2, z: 4, core: 2. Of those that a mesh axis runs over, the one named last changes fastest.
Arguments:
- fraction: float32 [3, 32768], P(None, ('wide', 'narrow')), may hold values from 0 to 1
- masses: float32 [32768], P(('wide', 'narrow')), may hold values from 0.05 to 0.5
- leaf_cell: int32 [3, 256], P(None, ('wide', 'narrow')), may hold values from 0 to 255, as said below
- exports: int32 [4, 64], P(None, ('wide', 'narrow')), may hold values from 0 to 8, as said below
- tile_lists: int32 [2, 256], P(None, ('wide', 'narrow')), may hold values from 0 to 7, as said below
Outputs:
- accel: float32 [3, 32768], P(None, ('wide', 'narrow'))
The draws below stay inside these ranges and needn't reach their ends.
Inputs may be any that keep to these rules, and one draw needn't show every extreme that they name: `leaf_cell`: column n belongs to rank m = n // 8, with wide index m // 4 and narrow index m mod 4: its first entry plus 0 .. 1 lies within that wide index's 32 planes, its second entry plus 0 .. 3 within that narrow index's 64 planes; the third entry is any cell. `exports`: row f and the 2 columns of rank m list distinct local leaf numbers of rank m to be exported across face f, then the value 8 in empty slots; every rank fills all slots of one of its rows. `tile_lists`: column n lists 2 distinct local leaf numbers of rank n // 8.
All inputs are finite; a program needn't handle non-finite values.
Results may differ from the reference program's by a relative error of at most 0.0003.
Values sent between devices are 32-bit elements; how exact they have to be, the bound alone decides.
A program may use at most 64 MiB of HBM per device.

```python
import math
import jax
import jax.numpy as jnp
from jax import lax

G = 256
LEAF = 128
PX = 2
PY = 4
PZ = 16
TILES = 2
LEAVES_DEV = 8
EXPORTS = 2
SLAB_X = 32
SLAB_Y = 64
COLUMNS = 4
RANKS = 32
PARTICLES = 32768
N_WIDE = 8
N_NARROW = 4


def layout(key):

    def per_rank(rank_index):
        subkeys = jax.random.split(jax.random.fold_in(key, rank_index), 6)
        slot_index = jnp.arange(LEAVES_DEV, dtype=jnp.int32)
        order_x = jax.random.permutation(subkeys[0], LEAVES_DEV).astype(jnp.int32)
        order_y = jax.random.permutation(subkeys[1], LEAVES_DEV).astype(jnp.int32)
        counts = jax.random.randint(subkeys[2], (4,), 1, EXPORTS + 1, dtype=jnp.int32)
        counts = jnp.where(jnp.arange(4, dtype=jnp.int32) == rank_index % 4, EXPORTS, counts)
        place_x = jnp.zeros((LEAVES_DEV,), jnp.int32).at[order_x].set(slot_index)
        place_y = jnp.zeros((LEAVES_DEV,), jnp.int32).at[order_y].set(slot_index)
        inner_x = jax.random.randint(subkeys[3], (LEAVES_DEV,), 1, SLAB_X - PX, dtype=jnp.int32)
        inner_y = jax.random.randint(subkeys[4], (LEAVES_DEV,), 1, SLAB_Y - PY, dtype=jnp.int32)
        base_x = jnp.where(place_x < counts[0], SLAB_X - PX, jnp.where((place_x >= EXPORTS) & (place_x < EXPORTS + counts[1]), 0, inner_x))
        base_y = jnp.where(place_y < counts[2], SLAB_Y - PY, jnp.where((place_y >= EXPORTS) & (place_y < EXPORTS + counts[3]), 0, inner_y))
        spacing = G // LEAVES_DEV
        base_z = slot_index * spacing + jax.random.randint(subkeys[5], (LEAVES_DEV,), 0, spacing, dtype=jnp.int32)
        wide_at = rank_index // COLUMNS
        narrow_at = rank_index % COLUMNS
        cell_table = jnp.stack([wide_at * SLAB_X + base_x, narrow_at * SLAB_Y + base_y, base_z]).astype(jnp.int32)
        column = jnp.arange(EXPORTS, dtype=jnp.int32)
        export_lists = jnp.stack([jnp.where(column < counts[0], order_x[column], LEAVES_DEV), jnp.where(column < counts[1], order_x[EXPORTS + column], LEAVES_DEV), jnp.where(column < counts[2], order_y[column], LEAVES_DEV), jnp.where(column < counts[3], order_y[EXPORTS + column], LEAVES_DEV)]).astype(jnp.int32)
        return (cell_table, export_lists)
    cell_table, export_lists = jax.vmap(per_rank)(jnp.arange(RANKS, dtype=jnp.int32))
    return (jnp.transpose(cell_table, (1, 0, 2)).reshape(3, -1), jnp.transpose(export_lists, (1, 0, 2)).reshape(4, -1))


def draw_leaf_cell(key, part):
    return layout(key)[0]


def draw_exports(key, part):
    return layout(key)[1]


def draw_tile_lists(key, part):
    leaf_total = RANKS * LEAVES_DEV
    subkeys = jax.random.split(jax.random.fold_in(key, 7), leaf_total)
    chosen = jax.vmap(lambda subkey: jax.random.permutation(subkey, TILES + 1)[:TILES])(subkeys).astype(jnp.int32)
    leaf_index = jnp.arange(leaf_total, dtype=jnp.int32) % LEAVES_DEV
    local_ids = (leaf_index[:, None] + chosen - TILES // 2) % LEAVES_DEV
    return jnp.transpose(local_ids).astype(jnp.int32)


def shard_levels(own_key, shape, cuts, low, top_value):
    level = 1.0
    for axis_at, parts in cuts:
        heights = jax.random.uniform(jax.random.fold_in(jax.random.fold_in(own_key, 6), axis_at), (parts,), jnp.float32, low / len(cuts), top_value / len(cuts))
        level = level * jnp.repeat(jnp.exp(heights), shape[axis_at] // parts).reshape((-1,) + (1,) * (len(shape) - 1 - axis_at))
    return level


def setup_inputs(seed: int = 0) -> dict:
    streams_of = jax.random.split(jax.random.key(seed), 6)
    return {
        "fraction": jnp.clip(1.0 * jax.random.uniform(streams_of[0], (3, PARTICLES), jnp.float32) ** shard_levels(streams_of[0], (3, PARTICLES), ((1, 32),), -0.2, 0.2), 0.0, 1.0),
        "masses": jnp.clip(jnp.exp(math.log(0.5) - 2.3025851 * jax.random.uniform(streams_of[1], (PARTICLES,), jnp.float32) ** shard_levels(streams_of[1], (PARTICLES,), ((0, 32),), -0.2, 0.2)), 0.05, 0.5),
        "leaf_cell": draw_leaf_cell(jax.random.fold_in(streams_of[5], 71), 0),
        "exports": draw_exports(jax.random.fold_in(streams_of[5], 71), 0),
        "tile_lists": draw_tile_lists(jax.random.fold_in(streams_of[5], 71), 0),
    }


SCREEN = 0.5
SOFTEN = 0.5
PRECISE = lax.Precision.HIGHEST

def cic_weights(fraction, extent):
    coordinate = 0.5 + fraction * (extent - 1.0)
    centres = jnp.arange(extent, dtype=jnp.int32).astype(jnp.float32) + 0.5
    return jnp.maximum(0.0, 1.0 - jnp.abs(coordinate[..., None] - centres))

def leaf_positions(cell_table, fraction):
    leaf_total = cell_table.shape[1]
    extents = jnp.asarray([PX - 1.0, PY - 1.0, PZ - 1.0], dtype=jnp.float32)
    scaled = fraction.reshape(3, leaf_total, -1) * extents[:, None, None] + 0.5
    return jnp.transpose(cell_table.astype(jnp.float32)[:, :, None] + scaled, (1, 0, 2))

def tile_block(targets, sources, masses):
    separation = sources[:, :, :, None, :] - targets[:, None, :, :, None]
    separation = separation - G * jnp.floor(separation / G + 0.5)
    squared = lax.optimization_barrier(jnp.sum(separation * separation, axis=2))
    distance = jnp.sqrt(squared)
    screened = jax.scipy.special.erfc(distance / (2.0 * SCREEN)) + distance / (SCREEN * math.sqrt(math.pi)) * jnp.exp(-squared / (4.0 * SCREEN * SCREEN))
    weight = masses[:, :, None, :] * screened / (squared + SOFTEN * SOFTEN) ** 1.5
    return lax.optimization_barrier(jnp.sum(weight[:, :, None, :, :] * separation, axis=(1, 4)))

def tile_forces(targets, sources, masses):
    block_size = 4
    blocks = targets.shape[0] // block_size

    def one_block(blocked):
        return tile_block(blocked[0], blocked[1], blocked[2])
    result = lax.map(one_block, (targets.reshape((blocks, block_size) + targets.shape[1:]), sources.reshape((blocks, block_size) + sources.shape[1:]), masses.reshape((blocks, block_size) + masses.shape[1:])))
    return result.reshape(targets.shape)

def green_factor(wave_x, wave_y, wave_z):
    squared_sum = 0.0
    for wavenumber in (wave_x, wave_y, wave_z):
        folded = jnp.where(wavenumber > G // 2, wavenumber - G, wavenumber).astype(jnp.float32) * (2.0 * math.pi / G)
        squared_sum = squared_sum + folded * folded
    divisor = jnp.where(squared_sum > 0, squared_sum, 1.0)
    return jnp.where(squared_sum > 0, -4.0 * math.pi * jnp.exp(-squared_sum * SCREEN * SCREEN) / divisor, 0.0)

def differences(potential, axis_index):
    return -(8.0 * (jnp.roll(potential, -1, axis_index) - jnp.roll(potential, 1, axis_index)) - (jnp.roll(potential, -2, axis_index) - jnp.roll(potential, 2, axis_index))) / 12.0

def reference(fraction, masses, leaf_cell, exports, tile_lists):
    ranks = leaf_cell.shape[1] // LEAVES_DEV
    positions = leaf_positions(leaf_cell, fraction)
    leaf_mass = masses.reshape(-1, LEAF)
    cell_x = leaf_cell[0][:, None] + jnp.arange(PX, dtype=jnp.int32)
    cell_y = leaf_cell[1][:, None] + jnp.arange(PY, dtype=jnp.int32)
    cell_z = (leaf_cell[2][:, None] + jnp.arange(PZ, dtype=jnp.int32)) % G
    fraction_leaf = fraction.reshape(3, -1, LEAF)
    weight_x = cic_weights(fraction_leaf[0], PX)
    weight_y = cic_weights(fraction_leaf[1], PY)
    weight_z = cic_weights(fraction_leaf[2], PZ)
    patch_mass = jnp.einsum('np,npa,npb,npc->nabc', leaf_mass, weight_x, weight_y, weight_z, precision=PRECISE)
    density = jnp.zeros((G, G, G), jnp.float32).at[cell_x[:, :, None, None], cell_y[:, None, :, None], cell_z[:, None, None, :]].add(patch_mass)
    spectrum = jnp.fft.fftn(density)
    waves = jnp.arange(G, dtype=jnp.int32)
    greens = green_factor(waves[:, None, None], waves[None, :, None], waves[None, None, :])
    potential = jnp.real(jnp.fft.ifftn(spectrum * greens))
    accel_field = jnp.stack([differences(potential, 0), differences(potential, 1), differences(potential, 2)])
    sampled = accel_field[:, cell_x[:, :, None, None], cell_y[:, None, :, None], cell_z[:, None, None, :]]
    long_range = jnp.einsum('knabc,npa,npb,npc->knp', sampled, weight_x, weight_y, weight_z, precision=PRECISE)
    by_rank = positions.reshape(ranks, LEAVES_DEV, 3, LEAF)
    mass_rank = leaf_mass.reshape(ranks, LEAVES_DEV, LEAF)
    lists_rank = jnp.transpose(tile_lists.reshape(TILES, ranks, LEAVES_DEV), (1, 2, 0))
    export_rank = jnp.transpose(exports.reshape(4, ranks, EXPORTS), (1, 0, 2))

    def per_rank(rank_index):
        own_leaves = by_rank[rank_index]
        own_mass = mass_rank[rank_index]
        own_lists = lists_rank[rank_index]
        result = tile_forces(own_leaves, own_leaves[own_lists], own_mass[own_lists])
        wide_at = rank_index // N_NARROW
        narrow_at = rank_index % N_NARROW
        neighbours = jnp.stack([(wide_at + 1) % N_WIDE * N_NARROW + narrow_at, (wide_at - 1) % N_WIDE * N_NARROW + narrow_at, wide_at * N_NARROW + (narrow_at + 1) % N_NARROW, wide_at * N_NARROW + (narrow_at - 1) % N_NARROW]).astype(jnp.int32)
        listed = export_rank[rank_index]
        chosen = jnp.minimum(listed, LEAVES_DEV - 1)
        filled = (listed < LEAVES_DEV).astype(jnp.float32)
        guest_lists = lists_rank[neighbours[:, None], chosen]
        sources = by_rank[neighbours[:, None, None], guest_lists]
        source_mass = mass_rank[neighbours[:, None, None], guest_lists]
        guests = own_leaves[chosen]
        forces = tile_forces(guests.reshape(4 * EXPORTS, 3, LEAF), sources.reshape(4 * EXPORTS, TILES, 3, LEAF), source_mass.reshape(4 * EXPORTS, TILES, LEAF))
        forces = forces.reshape(4, EXPORTS, 3, LEAF) * filled[:, :, None, None]
        return result.at[chosen.reshape(-1)].add(forces.reshape(4 * EXPORTS, 3, LEAF))
    short_range = lax.map(per_rank, jnp.arange(ranks, dtype=jnp.int32))
    short_range = jnp.transpose(short_range, (2, 0, 1, 3)).reshape(3, -1, LEAF)
    return (long_range + short_range).reshape(3, -1)
```

```python
import functools
import math

import jax
import jax.numpy as jnp
from jax import lax
from jax.experimental import pallas as pl
from jax.experimental.pallas import tpu as pltpu
from jax.sharding import PartitionSpec as P

G = 256
PX = 2
PY = 4
PZ = 16
PATCH_YZ = PY * PZ
PATCH = PX * PATCH_YZ
SCREEN = 0.5
SOFTEN = 0.5
ERFCX = (
    0.2820947416810428,
    0.28210427504184366,
    0.24651391069954823,
    0.18039116519942175,
    0.058372405908860704,
    0.0792320361696661,
    -0.1983246779625943,
    0.030722780905291756,
    0.06437369661731697,
    -0.025480486181070308,
)
VMEM = pl.BlockSpec(memory_space=pltpu.VMEM)
SMEM = pl.BlockSpec(memory_space=pltpu.SMEM)


def iota(shape, dim):
    return lax.broadcasted_iota(jnp.int32, shape, dim)


def sincos(count):
    quarters = count * (4.0 / G)
    near = jnp.floor(quarters + 0.5)
    z = (quarters - near) * (math.pi / 2)
    q = near.astype(jnp.int32)
    zz = z * z
    c = 1.0 + zz * (-0.5 + zz * (1.0 / 24 + zz * (-1.0 / 720 + zz * (1.0 / 40320))))
    s = z * (1.0 + zz * (-1.0 / 6 + zz * (1.0 / 120 + zz * (-1.0 / 5040))))
    swap = (q & 1) == 1
    cosine = jnp.where(swap, s, c)
    sine = jnp.where(swap, c, s)
    cosine = jnp.where(((q + 1) & 2) == 2, -cosine, cosine)
    sine = jnp.where((q & 2) == 2, -sine, sine)
    return cosine, sine


def split(x):
    hi = x.astype(jnp.bfloat16)
    return hi, (x - hi.astype(jnp.float32)).astype(jnp.bfloat16)


def dot3(left, right, dims=((1,), (0,))):
    dims = (dims, ((), ()))
    dot = functools.partial(
        lax.dot_general, dimension_numbers=dims, preferred_element_type=jnp.float32
    )
    return dot(left[0], right[0]) + (dot(left[0], right[1]) + dot(left[1], right[0]))


def folded(wave):
    return jnp.where(wave > G // 2, wave - G, wave).astype(jnp.float32)


def slope(wave):
    w = wave.astype(jnp.float32)
    return (8.0 * sincos(w)[1] - sincos(2.0 * w)[1]) * (1.0 / 6.0)


def leaf_weights(u):
    members = u.shape[1]
    row = iota((PATCH, members), 0)
    cells = (row // PATCH_YZ, row // PZ % PY, row % PZ)
    product = None
    for c, extent in enumerate((PX, PY, PZ)):
        centre = cells[c].astype(jnp.float32) + 0.5
        coordinate = 0.5 + u[c : c + 1] * (extent - 1.0)
        w = jnp.maximum(0.0, 1.0 - jnp.abs(coordinate - centre))
        product = w if product is None else product * w
    return product


def patch_kernel(fraction, masses, out):
    leaves, members = masses.shape
    m = masses[...]
    for n in range(leaves):
        w = leaf_weights(fraction[:, n * members : (n + 1) * members])
        out[n : n + 1, :] = dot3(split(m), split(w), ((1,), (1,)))[n : n + 1, :]


def mode_columns(base, rows, ny, origin):
    w = base + iota((rows, 1), 0)
    kz = origin[0] + w // ny
    ky = origin[1] + w % ny
    return ky, kz


def forward_kernel(ny, chunk, origin, patches, cells, out, e_hi, e_lo):
    step = pl.program_id(0)
    size = patches.shape[0]
    modes = out.shape[0]
    x_col = patches[:, PATCH : PATCH + 1]
    kx = iota((size, G), 1).astype(jnp.float32)
    for a in range(PX):
        c, s = sincos((x_col + float(a)) * kx)
        r0, r1 = a * size, (PX + a) * size
        for part, r, col in ((c, r0, 0), (-s, r0, G), (s, r1, 0), (c, r1, G)):
            hi, lo = split(part)
            e_hi[r : r + size, col : col + G] = hi
            e_lo[r : r + size, col : col + G] = lo
    y_row = cells[1:2, :]
    z_row = cells[2:3, :]

    def body(i, carry):
        at = pl.ds(pl.multiple_of(i * chunk, 8), chunk)
        ky, kz = mode_columns(i * chunk, chunk, ny, origin)
        kyf, kzf = ky.astype(jnp.float32), kz.astype(jnp.float32)
        lane = iota((1, PATCH_YZ), 1)
        tc, ts = sincos(
            kyf * (lane // PZ).astype(jnp.float32) + kzf * (lane % PZ).astype(jnp.float32)
        )
        tc, ts = split(tc), split(ts)
        c, s = sincos(kyf * y_row + kzf * z_row)
        real, imag = [], []
        for a in range(PX):
            p = split(patches[:, a * PATCH_YZ : (a + 1) * PATCH_YZ])
            fc = dot3(tc, p, ((1,), (1,)))
            fs = dot3(ts, p, ((1,), (1,)))
            real.append(fc * c - fs * s)
            imag.append(-(fc * s + fs * c))
        m = split(jnp.concatenate(real + imag, axis=1))
        got = dot3(m, (e_hi[...], e_lo[...]))

        @pl.when(step == 0)
        def _():
            out[at, :] = got

        @pl.when(step > 0)
        def _():
            out[at, :] += got

        @pl.when(step == pl.num_programs(0) - 1)
        def _():
            unit = 2.0 * math.pi / G
            fx = folded(iota((1, G), 1)) * unit
            fy, fz = folded(ky) * unit, folded(kz) * unit
            total = fx * fx + (fy * fy + fz * fz)
            divisor = jnp.where(total > 0, total, 1.0)
            green = jnp.where(
                total > 0, -4.0 * math.pi * jnp.exp(-total * (SCREEN * SCREEN)) / divisor, 0.0
            )
            for col in (0, G):
                out[at, col : col + G] = out[at, col : col + G] * green

        return carry

    lax.fori_loop(0, modes // chunk, body, 0)


def inverse_kernel(ny, chunk, origin, spectrum, cells, out, e_hi, e_lo, acc):
    size = cells.shape[1]
    modes = spectrum.shape[0]
    width = PX * size
    kx = iota((G, size), 0).astype(jnp.float32)
    for a in range(PX):
        c, s = sincos((cells[0:1, :] + float(a)) * kx)
        c0, c1 = a * size, (PX + a) * size
        for part, r, col in ((c, 0, c0), (s, 0, c1), (-s, G, c0), (c, G, c1)):
            hi, lo = split(part)
            e_hi[r : r + G, col : col + size] = hi
            e_lo[r : r + G, col : col + size] = lo
    y_row = cells[1:2, :]
    z_row = cells[2:3, :]
    acc[...] = jnp.zeros_like(acc)

    def body(i, carry):
        at = pl.ds(pl.multiple_of(i * chunk, 8), chunk)
        ky, kz = mode_columns(i * chunk, chunk, ny, origin)
        c, s = sincos(ky.astype(jnp.float32) * y_row + kz.astype(jnp.float32) * z_row)
        spec = spectrum[at, :]
        e = (e_hi[...], e_lo[...])
        lane_w = i * chunk + iota((1, chunk), 1)
        kz_row = origin[0] + lane_w // ny
        ky_row = origin[1] + lane_w % ny
        row = iota((PATCH_YZ, 1), 0)
        tc, ts = sincos(
            ky_row.astype(jnp.float32) * (row // PZ).astype(jnp.float32)
            + kz_row.astype(jnp.float32) * (row % PZ).astype(jnp.float32)
        )
        half = G // 2
        weight = jnp.where(
            (kz_row == 0) | (kz_row == half), 1.0, jnp.where(kz_row < half, 2.0, 0.0)
        ) * (1.0 / float(G * G * G))
        tc, ts = tc * weight, ts * weight
        dy, dz = slope(ky_row), slope(kz_row)

        def fields(source, cos_rows, sin_rows):
            p = dot3(split(source), e)
            total = None
            real, imag = [], []
            for a in range(PX):
                pr = p[:, a * size : (a + 1) * size]
                pi = p[:, (PX + a) * size : (PX + a + 1) * size]
                real.append(pr * c - pi * s)
                imag.append(pr * s + pi * c)
            real = split(jnp.concatenate(real, axis=1))
            imag = split(jnp.concatenate(imag, axis=1))
            return dot3(split(sin_rows), real) + dot3(split(cos_rows), imag)

        dx = slope(iota((1, 2 * G), 1) % G)
        acc[0:PATCH_YZ, :] += fields(spec * dx, tc, ts)
        acc[PATCH_YZ:, :] += fields(
            spec,
            jnp.concatenate([tc * dy, tc * dz], axis=0),
            jnp.concatenate([ts * dy, ts * dz], axis=0),
        )
        return carry

    lax.fori_loop(0, modes // chunk, body, 0)
    for f in range(3):
        for a in range(PX):
            block = acc[f * PATCH_YZ : (f + 1) * PATCH_YZ, a * size : (a + 1) * size]
            col = f * PATCH + a * PATCH_YZ
            out[:, col : col + PATCH_YZ] = block.T


def pair_kernel(leaves, jobs, source_at, target_at, shift, live, sources, out):
    out[...] = jnp.zeros_like(out)

    def body(j, carry):
        target = target_at[j]
        tgt = sources[target]
        total = [0.0, 0.0, 0.0]
        for k in range(2):
            src = sources[source_at[k, j]]
            cols = src.T
            members = src.shape[1]
            d = []
            for c in range(3):
                col = cols[:, c : c + 1] + shift[3 * k + c, j]
                d.append(jnp.broadcast_to(col, (members, members)) - tgt[c : c + 1, :])
            squared = d[0] * d[0] + d[1] * d[1] + d[2] * d[2]
            r = squared * lax.rsqrt(jnp.maximum(squared, 1e-30))
            t = 1.0 / (1.0 + 0.5 * r)
            poly = ERFCX[-1] * t + ERFCX[-2]
            for coefficient in ERFCX[-3::-1]:
                poly = poly * t + coefficient
            screened = jnp.exp(-squared) * (poly * t + (2.0 / math.sqrt(math.pi)) * r)
            inv = lax.rsqrt(squared + SOFTEN * SOFTEN)
            w = cols[:, 3:4] * screened * (inv * inv * inv)
            for c in range(3):
                total[c] = total[c] + jnp.sum(w * d[c], axis=0, keepdims=True)
        pick = live[j]
        out[target, 0:3, :] += jnp.concatenate(total, axis=0) * pick
        return carry

    lax.fori_loop(0, jobs, body, 0)


def sample_kernel(field, fraction, short, out):
    leaves = field.shape[0]
    members = fraction.shape[1] // leaves
    for n in range(leaves):
        at = slice(n * members, (n + 1) * members)
        w = split(leaf_weights(fraction[:, at]))
        values = jnp.concatenate(
            [field[n : n + 1, f * PATCH : (f + 1) * PATCH] for f in range(3)], axis=0
        )
        out[:, at] = dot3(split(values), w) + short[n, 0:3, :]


def local(fraction, masses, leaf_cell, exports, tile_lists):
    leaves = leaf_cell.shape[1]
    members = masses.shape[0] // leaves
    slots = exports.shape[1]
    n_wide, n_narrow = lax.axis_size("wide"), lax.axis_size("narrow")
    everyone = ("wide", "narrow")
    total = leaves * n_wide * n_narrow
    leaf_mass = masses.reshape(leaves, members)
    f32 = jnp.float32

    patch = pl.pallas_call(
        patch_kernel,
        out_shape=jax.ShapeDtypeStruct((leaves, PATCH), f32),
        in_specs=[VMEM, VMEM],
        out_specs=VMEM,
        name="patch",
    )(fraction, leaf_mass)
    cell_f = leaf_cell.astype(f32)
    packed = jnp.concatenate([patch, cell_f.T], axis=1)
    gathered = lax.all_gather(packed, everyone, axis=0, tiled=True)
    cells = gathered[:, PATCH : PATCH + 3].T

    extents = jnp.asarray([PX - 1.0, PY - 1.0, PZ - 1.0], dtype=f32)
    place = fraction.reshape(3, leaves, members) * extents[:, None, None] + 0.5
    place = jnp.transpose(cell_f[:, :, None] + place, (1, 0, 2))
    notes = jnp.concatenate([tile_lists.T.astype(f32), cell_f.T], axis=1)
    notes = jnp.pad(notes, ((0, 0), (0, members - notes.shape[1])))
    book = jnp.concatenate([place, leaf_mass[:, None], notes[:, None]], axis=1)
    books = [book]
    for axis, by in (("wide", -1), ("wide", 1), ("narrow", -1), ("narrow", 1)):
        peers = lax.axis_size(axis)
        books.append(lax.ppermute(book, axis, [(i, (i + by) % peers) for i in range(peers)]))
    books = jnp.stack(books)
    lists = books[:, :, 4, 0:2].astype(jnp.int32)
    corner = books[:, :, 4, 2:5]
    chosen = jnp.minimum(exports, leaves - 1).reshape(-1)
    target_at = jnp.concatenate([jnp.arange(leaves, dtype=jnp.int32), chosen])
    rank_at = jnp.concatenate(
        [jnp.zeros((leaves,), jnp.int32), jnp.repeat(jnp.arange(1, 5, dtype=jnp.int32), slots)]
    )
    live = jnp.concatenate([jnp.ones((leaves,), f32), (exports < leaves).astype(f32).reshape(-1)])
    source_at = rank_at[None, :] * leaves + lists[rank_at, target_at].T
    apart = corner.reshape(5 * leaves, 3)[source_at] - cell_f.T[target_at][None]
    shift = -float(G) * jnp.floor(apart / G + 0.5)
    shift = jnp.transpose(shift, (0, 2, 1)).reshape(6, -1)
    jobs = target_at.shape[0]
    sources = jnp.pad(books.reshape(5 * leaves, 5, members), ((0, 0), (0, 3), (0, 0)))
    short = pl.pallas_call(
        functools.partial(pair_kernel, leaves, jobs),
        out_shape=jax.ShapeDtypeStruct((leaves, 8, members), f32),
        in_specs=[SMEM, SMEM, SMEM, SMEM, VMEM],
        out_specs=VMEM,
        cost_estimate=pl.CostEstimate(
            flops=jobs * 2 * members * members * 60, bytes_accessed=2**20, transcendentals=0
        ),
        name="pairs",
    )(source_at, target_at, shift, live, sources)

    nz = -(-(G // 2 + 1) // n_narrow)
    ny = G // n_wide
    modes = nz * ny
    parts = next(p for p in range(1, modes + 1) if nz % p == 0 and modes // p <= 384)
    chunk = modes // parts
    origin = jnp.stack([lax.axis_index("narrow") * nz, lax.axis_index("wide") * ny]).astype(
        jnp.int32
    )
    size = min(total, 256)
    blocks = total // size
    params = pltpu.CompilerParams(vmem_limit_bytes=56 * 2**20)
    spectrum = pl.pallas_call(
        functools.partial(forward_kernel, ny, chunk),
        grid=(blocks,),
        out_shape=jax.ShapeDtypeStruct((modes, 2 * G), f32),
        in_specs=[
            SMEM,
            pl.BlockSpec((size, PATCH + 3), lambda i: (i, 0)),
            pl.BlockSpec((3, size), lambda i: (0, i)),
        ],
        out_specs=pl.BlockSpec((modes, 2 * G), lambda i: (0, 0)),
        scratch_shapes=[
            pltpu.VMEM((2 * PX * size, 2 * G), jnp.bfloat16),
            pltpu.VMEM((2 * PX * size, 2 * G), jnp.bfloat16),
        ],
        compiler_params=params,
        name="forward",
    )(origin, gathered, cells)
    partial = pl.pallas_call(
        functools.partial(inverse_kernel, ny, chunk),
        grid=(blocks,),
        out_shape=jax.ShapeDtypeStruct((total, 3 * PATCH), f32),
        in_specs=[
            SMEM,
            pl.BlockSpec((modes, 2 * G), lambda i: (0, 0)),
            pl.BlockSpec((3, size), lambda i: (0, i)),
        ],
        out_specs=pl.BlockSpec((size, 3 * PATCH), lambda i: (i, 0)),
        scratch_shapes=[
            pltpu.VMEM((2 * G, 2 * PX * size), jnp.bfloat16),
            pltpu.VMEM((2 * G, 2 * PX * size), jnp.bfloat16),
            pltpu.VMEM((3 * PATCH_YZ, PX * size), f32),
        ],
        compiler_params=params,
        name="inverse",
    )(origin, spectrum, cells)
    field = lax.psum_scatter(partial, everyone, scatter_dimension=0, tiled=True)
    return pl.pallas_call(
        sample_kernel,
        out_shape=jax.ShapeDtypeStruct((3, leaves * members), f32),
        in_specs=[VMEM, VMEM, VMEM],
        out_specs=VMEM,
        name="sample",
    )(field, fraction, short)


def solution(mesh):
    placed = (
        P(None, ("wide", "narrow")),
        P(("wide", "narrow")),
        P(None, ("wide", "narrow")),
        P(None, ("wide", "narrow")),
        P(None, ("wide", "narrow")),
    )
    return jax.shard_map(
        local, mesh=mesh, in_specs=placed, out_specs=P(None, ("wide", "narrow")), check_vma=False
    )
```

```python
import functools
import math

import jax
import jax.numpy as jnp
from jax import lax
from jax.experimental import pallas as pl
from jax.experimental.pallas import tpu as pltpu
from jax.sharding import PartitionSpec as P

G = 256
PX = 2
PY = 4
PZ = 16
PATCH_YZ = PY * PZ
PATCH = PX * PATCH_YZ
SCREEN = 0.5
SOFTEN = 0.5
ERFCX = (
    0.2820947416810428,
    0.28210427504184366,
    0.24651391069954823,
    0.18039116519942175,
    0.058372405908860704,
    0.0792320361696661,
    -0.1983246779625943,
    0.030722780905291756,
    0.06437369661731697,
    -0.025480486181070308,
)
VMEM = pl.BlockSpec(memory_space=pltpu.VMEM)
SMEM = pl.BlockSpec(memory_space=pltpu.SMEM)


def iota(shape, dim):
    return lax.broadcasted_iota(jnp.int32, shape, dim)


def sincos(count):
    quarters = count * (4.0 / G)
    near = jnp.floor(quarters + 0.5)
    z = (quarters - near) * (math.pi / 2)
    q = near.astype(jnp.int32)
    zz = z * z
    c = 1.0 + zz * (-0.5 + zz * (1.0 / 24 + zz * (-1.0 / 720 + zz * (1.0 / 40320))))
    s = z * (1.0 + zz * (-1.0 / 6 + zz * (1.0 / 120 + zz * (-1.0 / 5040))))
    swap = (q & 1) == 1
    cosine = jnp.where(swap, s, c)
    sine = jnp.where(swap, c, s)
    cosine = jnp.where(((q + 1) & 2) == 2, -cosine, cosine)
    sine = jnp.where((q & 2) == 2, -sine, sine)
    return cosine, sine


def split(x):
    hi = x.astype(jnp.bfloat16)
    return hi, (x - hi.astype(jnp.float32)).astype(jnp.bfloat16)


def dot3(left, right, dims=((1,), (0,))):
    dims = (dims, ((), ()))
    dot = functools.partial(
        lax.dot_general, dimension_numbers=dims, preferred_element_type=jnp.float32
    )
    return dot(left[0], right[0]) + (dot(left[0], right[1]) + dot(left[1], right[0]))


def folded(wave):
    return jnp.where(wave > G // 2, wave - G, wave).astype(jnp.float32)


def slope(wave):
    w = wave.astype(jnp.float32)
    return (8.0 * sincos(w)[1] - sincos(2.0 * w)[1]) * (1.0 / 6.0)


def leaf_weights(u):
    members = u.shape[1]
    row = iota((PATCH, members), 0)
    cells = (row // PATCH_YZ, row // PZ % PY, row % PZ)
    product = None
    for c, extent in enumerate((PX, PY, PZ)):
        centre = cells[c].astype(jnp.float32) + 0.5
        coordinate = 0.5 + u[c : c + 1] * (extent - 1.0)
        w = jnp.maximum(0.0, 1.0 - jnp.abs(coordinate - centre))
        product = w if product is None else product * w
    return product


def pack_kernel(leaf_cell, tile_lists, fraction, masses, packed, book):
    leaves = packed.shape[0]
    members = masses.shape[1] // leaves
    lane = iota((1, members), 1)
    for n in range(leaves):
        at = slice(n * members, (n + 1) * members)
        u = fraction[:, at]
        m = masses[:, at]
        w = leaf_weights(u)
        full = jnp.broadcast_to(m, (8, members))
        packed[n : n + 1, 0:PATCH] = dot3(split(full), split(w), ((1,), (1,)))[0:1, :]
        cell = [leaf_cell[c, n].astype(jnp.float32) for c in range(3)]
        note = jnp.zeros((1, members), jnp.float32)
        for c in range(3):
            note = jnp.where(lane == c, cell[c], note)
        packed[n : n + 1, PATCH:] = note[:, 0:PATCH]
        for k in range(2):
            note = jnp.where(lane == 3 + k, tile_lists[k, n].astype(jnp.float32), note)
        for c, extent in enumerate((PX, PY, PZ)):
            book[n, c : c + 1, :] = cell[c] + (u[c : c + 1] * (extent - 1.0) + 0.5)
        book[n, 3:4, :] = m
        book[n, 4:5, :] = note
        book[n, 5:8, :] = jnp.zeros((3, members), jnp.float32)


def peers_of(axis):
    count = lax.axis_size(axis)
    me = lax.axis_index(axis)
    return [(axis, s, lax.rem(me + s, count), lax.rem(me + count - s, count)) for s in range(1, count)]


def greet(groups):
    barrier = pltpu.get_barrier_semaphore()
    for axis, _, ahead, _ in groups:
        pl.semaphore_signal(
            barrier, inc=1, device_id={axis: ahead}, device_id_type=pl.DeviceIdType.MESH
        )
    pl.semaphore_wait(barrier, len(groups))


def remote(src, dst, send, recv, axis, to):
    return pltpu.make_async_remote_copy(
        src_ref=src,
        dst_ref=dst,
        send_sem=send,
        recv_sem=recv,
        device_id={axis: to},
        device_id_type=pl.DeviceIdType.MESH,
    )


def gather_kernel(packed, book, out, books, own, sends, recvs):
    wide, narrow = peers_of("wide"), peers_of("narrow")
    w, v = lax.axis_index("wide"), lax.axis_index("narrow")
    keep = [
        pltpu.make_async_copy(packed, out.at[w, v], own.at[0]),
        pltpu.make_async_copy(book, books.at[0], own.at[1]),
    ]
    for copy in keep:
        copy.start()
    greet(wide + narrow)
    at = 0
    first = []
    for axis, s, ahead, _ in narrow:
        first.append(remote(packed, out.at[w, v], sends.at[at], recvs.at[at], axis, ahead))
        at += 1
    for copy in first:
        copy.start()
    near = []
    for slot, (axis, to) in enumerate(
        (
            ("wide", wide[-1][2]),
            ("wide", wide[0][2]),
            ("narrow", narrow[-1][2]),
            ("narrow", narrow[0][2]),
        )
    ):
        near.append(remote(book, books.at[slot + 1], sends.at[at], recvs.at[at], axis, to))
        at += 1
    for copy in keep:
        copy.wait()
    for copy, (axis, s, _, behind) in zip(first, narrow):
        remote(
            packed, out.at[w, behind], sends.at[s - 1], recvs.at[s - 1], axis, behind
        ).wait_recv()
    second = []
    base = at
    for axis, s, ahead, _ in wide:
        second.append(remote(out.at[w], out.at[w], sends.at[at], recvs.at[at], axis, ahead))
        at += 1
    for copy in second + near:
        copy.start()
    for axis, s, _, behind in wide:
        i = base + s - 1
        remote(out.at[w], out.at[behind], sends.at[i], recvs.at[i], axis, behind).wait_recv()
    for copy in near:
        copy.wait_recv()
    for copy in first + second + near:
        copy.wait_send()


def scatter_kernel(partial, out, landed, mine, near, sends, recvs):
    wide, narrow = peers_of("wide"), peers_of("narrow")
    w, v = lax.axis_index("wide"), lax.axis_index("narrow")
    greet(wide + narrow)
    at = 0
    first = []
    for axis, s, ahead, _ in wide:
        first.append(
            remote(partial.at[ahead], landed.at[s - 1], sends.at[at], recvs.at[at], axis, ahead)
        )
        at += 1
    for copy in first:
        copy.start()
    for copy in first:
        copy.wait_recv()
    total = partial[w]
    for s in range(len(wide)):
        total = total + landed[s]
    mine[...] = total
    second = []
    for axis, s, ahead, _ in narrow:
        second.append(
            remote(mine.at[ahead], near.at[s - 1], sends.at[at], recvs.at[at], axis, ahead)
        )
        at += 1
    for copy in second:
        copy.start()
    for copy in second:
        copy.wait_recv()
    total = mine[v]
    for s in range(len(narrow)):
        total = total + near[s]
    out[...] = total
    for copy in first + second:
        copy.wait_send()


def mode_columns(base, rows, ny, origin):
    w = base + iota((rows, 1), 0)
    kz = origin[0] + w // ny
    ky = origin[1] + w % ny
    return ky, kz


def forward_kernel(ny, chunk, origin, patches, out, e_hi, e_lo):
    step = pl.program_id(0)
    size = patches.shape[0]
    modes = out.shape[0]
    x_col = patches[:, PATCH : PATCH + 1]
    kx = iota((size, G), 1).astype(jnp.float32)
    for a in range(PX):
        c, s = sincos((x_col + float(a)) * kx)
        r0, r1 = a * size, (PX + a) * size
        for part, r, col in ((c, r0, 0), (-s, r0, G), (s, r1, 0), (c, r1, G)):
            hi, lo = split(part)
            e_hi[r : r + size, col : col + G] = hi
            e_lo[r : r + size, col : col + G] = lo
    cells = patches[:, PATCH:].T
    y_row = cells[1:2, :]
    z_row = cells[2:3, :]

    def body(i, carry):
        at = pl.ds(pl.multiple_of(i * chunk, 8), chunk)
        ky, kz = mode_columns(i * chunk, chunk, ny, origin)
        kyf, kzf = ky.astype(jnp.float32), kz.astype(jnp.float32)
        lane = iota((1, PATCH_YZ), 1)
        tc, ts = sincos(
            kyf * (lane // PZ).astype(jnp.float32) + kzf * (lane % PZ).astype(jnp.float32)
        )
        tc, ts = split(tc), split(ts)
        c, s = sincos(kyf * y_row + kzf * z_row)
        real, imag = [], []
        for a in range(PX):
            p = split(patches[:, a * PATCH_YZ : (a + 1) * PATCH_YZ])
            fc = dot3(tc, p, ((1,), (1,)))
            fs = dot3(ts, p, ((1,), (1,)))
            real.append(fc * c - fs * s)
            imag.append(-(fc * s + fs * c))
        m = split(jnp.concatenate(real + imag, axis=1))
        got = dot3(m, (e_hi[...], e_lo[...]))

        @pl.when(step == 0)
        def _():
            out[at, :] = got

        @pl.when(step > 0)
        def _():
            out[at, :] += got

        @pl.when(step == pl.num_programs(0) - 1)
        def _():
            unit = 2.0 * math.pi / G
            fx = folded(iota((1, G), 1)) * unit
            fy, fz = folded(ky) * unit, folded(kz) * unit
            total = fx * fx + (fy * fy + fz * fz)
            divisor = jnp.where(total > 0, total, 1.0)
            green = jnp.where(
                total > 0, -4.0 * math.pi * jnp.exp(-total * (SCREEN * SCREEN)) / divisor, 0.0
            )
            for col in (0, G):
                out[at, col : col + G] = out[at, col : col + G] * green

        return carry

    lax.fori_loop(0, modes // chunk, body, 0)


def inverse_kernel(ny, chunk, origin, spectrum, leaf_rows, out, e_hi, e_lo, acc):
    size = leaf_rows.shape[0]
    cells = leaf_rows[:, PATCH:].T
    modes = spectrum.shape[0]
    width = PX * size
    kx = iota((G, size), 0).astype(jnp.float32)
    for a in range(PX):
        c, s = sincos((cells[0:1, :] + float(a)) * kx)
        c0, c1 = a * size, (PX + a) * size
        for part, r, col in ((c, 0, c0), (s, 0, c1), (-s, G, c0), (c, G, c1)):
            hi, lo = split(part)
            e_hi[r : r + G, col : col + size] = hi
            e_lo[r : r + G, col : col + size] = lo
    y_row = cells[1:2, :]
    z_row = cells[2:3, :]
    acc[...] = jnp.zeros_like(acc)

    def body(i, carry):
        at = pl.ds(pl.multiple_of(i * chunk, 8), chunk)
        ky, kz = mode_columns(i * chunk, chunk, ny, origin)
        c, s = sincos(ky.astype(jnp.float32) * y_row + kz.astype(jnp.float32) * z_row)
        spec = spectrum[at, :]
        e = (e_hi[...], e_lo[...])
        lane_w = i * chunk + iota((1, chunk), 1)
        kz_row = origin[0] + lane_w // ny
        ky_row = origin[1] + lane_w % ny
        row = iota((PATCH_YZ, 1), 0)
        tc, ts = sincos(
            ky_row.astype(jnp.float32) * (row // PZ).astype(jnp.float32)
            + kz_row.astype(jnp.float32) * (row % PZ).astype(jnp.float32)
        )
        half = G // 2
        weight = jnp.where(
            (kz_row == 0) | (kz_row == half), 1.0, jnp.where(kz_row < half, 2.0, 0.0)
        ) * (1.0 / float(G * G * G))
        tc, ts = tc * weight, ts * weight
        dy, dz = slope(ky_row), slope(kz_row)

        def fields(source, cos_rows, sin_rows):
            p = dot3(split(source), e)
            total = None
            real, imag = [], []
            for a in range(PX):
                pr = p[:, a * size : (a + 1) * size]
                pi = p[:, (PX + a) * size : (PX + a + 1) * size]
                real.append(pr * c - pi * s)
                imag.append(pr * s + pi * c)
            real = split(jnp.concatenate(real, axis=1))
            imag = split(jnp.concatenate(imag, axis=1))
            return dot3(split(sin_rows), real) + dot3(split(cos_rows), imag)

        dx = slope(iota((1, 2 * G), 1) % G)
        acc[0:PATCH_YZ, :] += fields(spec * dx, tc, ts)
        acc[PATCH_YZ:, :] += fields(
            spec,
            jnp.concatenate([tc * dy, tc * dz], axis=0),
            jnp.concatenate([ts * dy, ts * dz], axis=0),
        )
        return carry

    lax.fori_loop(0, modes // chunk, body, 0)
    for f in range(3):
        for a in range(PX):
            block = acc[f * PATCH_YZ : (f + 1) * PATCH_YZ, a * size : (a + 1) * size]
            col = f * PATCH + a * PATCH_YZ
            out[:, col : col + PATCH_YZ] = block.T


def pair_kernel(leaves, slots, exports, notes, books, out):
    out[...] = jnp.zeros_like(out)

    def job(rank, target, pick):
        tgt = books[0, target]
        total = [0.0, 0.0, 0.0]
        for k in range(2):
            source = notes[rank, target, 3 + k]
            src = books[rank, source]
            cols = src.T
            members = src.shape[1]
            d = []
            for c in range(3):
                apart = (notes[rank, source, c] - notes[0, target, c]).astype(jnp.float32)
                wraps = (apart > 0.5 * G).astype(jnp.int32) - (apart <= -0.5 * G).astype(jnp.int32)
                col = cols[:, c : c + 1] - float(G) * wraps.astype(jnp.float32)
                d.append(jnp.broadcast_to(col, (members, members)) - tgt[c : c + 1, :])
            squared = d[0] * d[0] + d[1] * d[1] + d[2] * d[2]
            r = squared * lax.rsqrt(jnp.maximum(squared, 1e-30))
            t = 1.0 / (1.0 + 0.5 * r)
            poly = ERFCX[-1] * t + ERFCX[-2]
            for coefficient in ERFCX[-3::-1]:
                poly = poly * t + coefficient
            screened = jnp.exp(-squared) * (poly * t + (2.0 / math.sqrt(math.pi)) * r)
            inv = lax.rsqrt(squared + SOFTEN * SOFTEN)
            w = cols[:, 3:4] * screened * (inv * inv * inv)
            for c in range(3):
                total[c] = total[c] + jnp.sum(w * d[c], axis=0, keepdims=True)
        out[target, 0:3, :] += jnp.concatenate(total, axis=0) * pick

    def own(n, carry):
        job(0, n, 1.0)
        return carry

    def guest(j, carry):
        face = j // slots
        leaf = exports[face, j % slots]
        job(face + 1, jnp.minimum(leaf, leaves - 1), (leaf < leaves).astype(jnp.float32))
        return carry

    lax.fori_loop(0, leaves, own, 0)
    lax.fori_loop(0, 4 * slots, guest, 0)


def sample_kernel(field, fraction, short, out):
    leaves = field.shape[0]
    members = fraction.shape[1] // leaves
    for n in range(leaves):
        at = slice(n * members, (n + 1) * members)
        w = split(leaf_weights(fraction[:, at]))
        values = jnp.concatenate(
            [field[n : n + 1, f * PATCH : (f + 1) * PATCH] for f in range(3)], axis=0
        )
        out[:, at] = dot3(split(values), w) + short[n, 0:3, :]


def local(fraction, masses, leaf_cell, exports, tile_lists):
    leaves = leaf_cell.shape[1]
    members = masses.shape[0] // leaves
    slots = exports.shape[1]
    n_wide, n_narrow = lax.axis_size("wide"), lax.axis_size("narrow")
    total = leaves * n_wide * n_narrow
    f32 = jnp.float32

    packed, book = pl.pallas_call(
        pack_kernel,
        out_shape=(
            jax.ShapeDtypeStruct((leaves, 2 * PATCH), f32),
            jax.ShapeDtypeStruct((leaves, 8, members), f32),
        ),
        in_specs=[SMEM, SMEM, VMEM, VMEM],
        out_specs=(VMEM, VMEM),
        name="pack",
    )(leaf_cell, tile_lists, fraction, masses.reshape(1, -1))
    copies = n_wide - 1 + n_narrow - 1
    gathered, books = pl.pallas_call(
        gather_kernel,
        out_shape=(
            jax.ShapeDtypeStruct((n_wide, n_narrow, leaves, 2 * PATCH), f32),
            jax.ShapeDtypeStruct((5, leaves, 8, members), f32),
        ),
        in_specs=[VMEM, VMEM],
        out_specs=(VMEM, VMEM),
        scratch_shapes=[
            pltpu.SemaphoreType.DMA((2,)),
            pltpu.SemaphoreType.DMA((copies + 4,)),
            pltpu.SemaphoreType.DMA((copies + 4,)),
        ],
        compiler_params=pltpu.CompilerParams(collective_id=0, has_side_effects=True),
        name="gather",
    )(packed, book)
    gathered = gathered.reshape(total, 2 * PATCH)
    notes = books[:, :, 4, 0:5].astype(jnp.int32)
    short = pl.pallas_call(
        functools.partial(pair_kernel, leaves, slots),
        out_shape=jax.ShapeDtypeStruct((leaves, 8, members), f32),
        in_specs=[SMEM, SMEM, VMEM],
        out_specs=VMEM,
        name="pairs",
    )(exports, notes, books)

    nz = -(-(G // 2 + 1) // n_narrow)
    ny = G // n_wide
    modes = nz * ny
    parts = next(p for p in range(1, modes + 1) if nz % p == 0 and modes // p <= 384)
    chunk = modes // parts
    origin = jnp.stack([lax.axis_index("narrow") * nz, lax.axis_index("wide") * ny]).astype(
        jnp.int32
    )
    size = min(total, 256)
    blocks = total // size
    params = pltpu.CompilerParams(vmem_limit_bytes=56 * 2**20)
    spectrum = pl.pallas_call(
        functools.partial(forward_kernel, ny, chunk),
        grid=(blocks,),
        out_shape=jax.ShapeDtypeStruct((modes, 2 * G), f32),
        in_specs=[
            SMEM,
            pl.BlockSpec((size, 2 * PATCH), lambda i: (i, 0)),
        ],
        out_specs=pl.BlockSpec((modes, 2 * G), lambda i: (0, 0)),
        scratch_shapes=[
            pltpu.VMEM((2 * PX * size, 2 * G), jnp.bfloat16),
            pltpu.VMEM((2 * PX * size, 2 * G), jnp.bfloat16),
        ],
        compiler_params=params,
        name="forward",
    )(origin, gathered)
    partial = pl.pallas_call(
        functools.partial(inverse_kernel, ny, chunk),
        grid=(blocks,),
        out_shape=jax.ShapeDtypeStruct((total, 3 * PATCH), f32),
        in_specs=[
            SMEM,
            pl.BlockSpec((modes, 2 * G), lambda i: (0, 0)),
            pl.BlockSpec((size, 2 * PATCH), lambda i: (i, 0)),
        ],
        out_specs=pl.BlockSpec((size, 3 * PATCH), lambda i: (i, 0)),
        scratch_shapes=[
            pltpu.VMEM((2 * G, 2 * PX * size), jnp.bfloat16),
            pltpu.VMEM((2 * G, 2 * PX * size), jnp.bfloat16),
            pltpu.VMEM((3 * PATCH_YZ, PX * size), f32),
        ],
        compiler_params=params,
        name="inverse",
    )(origin, spectrum, gathered)
    block = (leaves, 3 * PATCH)
    field = pl.pallas_call(
        scatter_kernel,
        out_shape=jax.ShapeDtypeStruct(block, f32),
        in_specs=[VMEM],
        out_specs=VMEM,
        scratch_shapes=[
            pltpu.VMEM((n_wide - 1, n_narrow) + block, f32),
            pltpu.VMEM((n_narrow,) + block, f32),
            pltpu.VMEM((n_narrow - 1,) + block, f32),
            pltpu.SemaphoreType.DMA((copies,)),
            pltpu.SemaphoreType.DMA((copies,)),
        ],
        compiler_params=pltpu.CompilerParams(collective_id=1, has_side_effects=True),
        name="scatter",
    )(partial.reshape((n_wide, n_narrow) + block))
    return pl.pallas_call(
        sample_kernel,
        out_shape=jax.ShapeDtypeStruct((3, leaves * members), f32),
        in_specs=[VMEM, VMEM, VMEM],
        out_specs=VMEM,
        name="sample",
    )(field, fraction, short)


def solution(mesh):
    placed = (
        P(None, ("wide", "narrow")),
        P(("wide", "narrow")),
        P(None, ("wide", "narrow")),
        P(None, ("wide", "narrow")),
        P(None, ("wide", "narrow")),
    )
    return jax.shard_map(
        local, mesh=mesh, in_specs=placed, out_specs=P(None, ("wide", "narrow")), check_vma=False
    )
```

```python
import functools
import math

import jax
import jax.numpy as jnp
from jax import lax
from jax.experimental import pallas as pl
from jax.experimental.pallas import tpu as pltpu
from jax.sharding import PartitionSpec as P

G = 256
PX = 2
PY = 4
PZ = 16
PATCH_YZ = PY * PZ
PATCH = PX * PATCH_YZ
SCREEN = 0.5
SOFTEN = 0.5
ERFCX = (
    0.2820947416810428,
    0.28210427504184366,
    0.24651391069954823,
    0.18039116519942175,
    0.058372405908860704,
    0.0792320361696661,
    -0.1983246779625943,
    0.030722780905291756,
    0.06437369661731697,
    -0.025480486181070308,
)
VMEM = pl.BlockSpec(memory_space=pltpu.VMEM)
SMEM = pl.BlockSpec(memory_space=pltpu.SMEM)


def iota(shape, dim):
    return lax.broadcasted_iota(jnp.int32, shape, dim)


def sincos(count):
    quarters = count * (4.0 / G)
    near = jnp.floor(quarters + 0.5)
    z = (quarters - near) * (math.pi / 2)
    q = near.astype(jnp.int32)
    zz = z * z
    c = 1.0 + zz * (-0.5 + zz * (1.0 / 24 + zz * (-1.0 / 720 + zz * (1.0 / 40320))))
    s = z * (1.0 + zz * (-1.0 / 6 + zz * (1.0 / 120 + zz * (-1.0 / 5040))))
    swap = (q & 1) == 1
    cosine = jnp.where(swap, s, c)
    sine = jnp.where(swap, c, s)
    cosine = jnp.where(((q + 1) & 2) == 2, -cosine, cosine)
    sine = jnp.where((q & 2) == 2, -sine, sine)
    return cosine, sine


def split(x):
    hi = x.astype(jnp.bfloat16)
    return hi, (x - hi.astype(jnp.float32)).astype(jnp.bfloat16)


def dot3(left, right, dims=((1,), (0,))):
    dims = (dims, ((), ()))
    dot = functools.partial(
        lax.dot_general, dimension_numbers=dims, preferred_element_type=jnp.float32
    )
    return dot(left[0], right[0]) + (dot(left[0], right[1]) + dot(left[1], right[0]))


def folded(wave):
    return jnp.where(wave > G // 2, wave - G, wave).astype(jnp.float32)


def slope(wave):
    w = wave.astype(jnp.float32)
    return (8.0 * sincos(w)[1] - sincos(2.0 * w)[1]) * (1.0 / 6.0)


def leaf_weights(u):
    members = u.shape[1]
    row = iota((PATCH, members), 0)
    cells = (row // PATCH_YZ, row // PZ % PY, row % PZ)
    product = None
    for c, extent in enumerate((PX, PY, PZ)):
        centre = cells[c].astype(jnp.float32) + 0.5
        coordinate = 0.5 + u[c : c + 1] * (extent - 1.0)
        w = jnp.maximum(0.0, 1.0 - jnp.abs(coordinate - centre))
        product = w if product is None else product * w
    return product


def pack_kernel(leaf_cell, tile_lists, fraction, masses, packed, book):
    leaves = packed.shape[0]
    members = masses.shape[1] // leaves
    lane = iota((1, members), 1)
    for n in range(leaves):
        at = slice(n * members, (n + 1) * members)
        u = fraction[:, at]
        m = masses[:, at]
        w = leaf_weights(u)
        full = jnp.broadcast_to(m, (8, members))
        packed[n : n + 1, 0:PATCH] = dot3(split(full), split(w), ((1,), (1,)))[0:1, :]
        cell = [leaf_cell[c, n].astype(jnp.float32) for c in range(3)]
        note = jnp.zeros((1, members), jnp.float32)
        for c in range(3):
            note = jnp.where(lane == c, cell[c], note)
        packed[n : n + 1, PATCH:] = note[:, 0:PATCH]
        for k in range(2):
            note = jnp.where(lane == 3 + k, tile_lists[k, n].astype(jnp.float32), note)
        for c, extent in enumerate((PX, PY, PZ)):
            book[n, c : c + 1, :] = cell[c] + (u[c : c + 1] * (extent - 1.0) + 0.5)
        book[n, 3:4, :] = m
        book[n, 4:5, :] = note
        book[n, 5:8, :] = jnp.zeros((3, members), jnp.float32)


def peers_of(axis):
    count = lax.axis_size(axis)
    me = lax.axis_index(axis)
    return [(axis, s, lax.rem(me + s, count), lax.rem(me + count - s, count)) for s in range(1, count)]


def greet(groups):
    barrier = pltpu.get_barrier_semaphore()
    for axis, _, ahead, _ in groups:
        pl.semaphore_signal(
            barrier, inc=1, device_id={axis: ahead}, device_id_type=pl.DeviceIdType.MESH
        )
    pl.semaphore_wait(barrier, len(groups))


def remote(src, dst, send, recv, axis, to):
    return pltpu.make_async_remote_copy(
        src_ref=src,
        dst_ref=dst,
        send_sem=send,
        recv_sem=recv,
        device_id={axis: to},
        device_id_type=pl.DeviceIdType.MESH,
    )


def gather_kernel(packed, book, out, books, own, sends, recvs):
    wide, narrow = peers_of("wide"), peers_of("narrow")
    w, v = lax.axis_index("wide"), lax.axis_index("narrow")
    keep = [
        pltpu.make_async_copy(packed, out.at[w, v], own.at[0]),
        pltpu.make_async_copy(book, books.at[0], own.at[1]),
    ]
    for copy in keep:
        copy.start()
    greet(wide + narrow)
    at = 0
    first = []
    for axis, s, ahead, _ in narrow:
        first.append(remote(packed, out.at[w, v], sends.at[at], recvs.at[at], axis, ahead))
        at += 1
    for copy in first:
        copy.start()
    near = []
    for slot, (axis, to) in enumerate(
        (
            ("wide", wide[-1][2]),
            ("wide", wide[0][2]),
            ("narrow", narrow[-1][2]),
            ("narrow", narrow[0][2]),
        )
    ):
        near.append(remote(book, books.at[slot + 1], sends.at[at], recvs.at[at], axis, to))
        at += 1
    for copy in keep:
        copy.wait()
    for copy, (axis, s, _, behind) in zip(first, narrow):
        remote(
            packed, out.at[w, behind], sends.at[s - 1], recvs.at[s - 1], axis, behind
        ).wait_recv()
    second = []
    base = at
    for axis, s, ahead, _ in wide:
        second.append(remote(out.at[w], out.at[w], sends.at[at], recvs.at[at], axis, ahead))
        at += 1
    for copy in second + near:
        copy.start()
    for axis, s, _, behind in wide:
        i = base + s - 1
        remote(out.at[w], out.at[behind], sends.at[i], recvs.at[i], axis, behind).wait_recv()
    for copy in near:
        copy.wait_recv()
    for copy in first + second + near:
        copy.wait_send()


def scatter_kernel(partial, out, landed, mine, near, sends, recvs):
    wide, narrow = peers_of("wide"), peers_of("narrow")
    w, v = lax.axis_index("wide"), lax.axis_index("narrow")
    greet(wide + narrow)
    at = 0
    first = []
    for axis, s, ahead, _ in wide:
        first.append(
            remote(partial.at[ahead], landed.at[s - 1], sends.at[at], recvs.at[at], axis, ahead)
        )
        at += 1
    for copy in first:
        copy.start()
    for copy in first:
        copy.wait_recv()
    total = partial[w]
    for s in range(len(wide)):
        total = total + landed[s]
    mine[...] = total
    second = []
    for axis, s, ahead, _ in narrow:
        second.append(
            remote(mine.at[ahead], near.at[s - 1], sends.at[at], recvs.at[at], axis, ahead)
        )
        at += 1
    for copy in second:
        copy.start()
    for copy in second:
        copy.wait_recv()
    total = mine[v]
    for s in range(len(narrow)):
        total = total + near[s]
    out[...] = total
    for copy in first + second:
        copy.wait_send()


def modes_at(index, ny, origin):
    return origin[1] + index % ny, origin[0] + index // ny


def x_basis(x, lane):
    half = G // 2
    wave = jnp.where(lane > half, lane - half, lane).astype(jnp.float32)
    turn = jnp.where(lane > half, float(G // 4), 0.0)
    return sincos(x * wave - turn)[0]


def forward_tables(patches, e_hi, e_lo, p_cat):
    size = patches.shape[0]
    x_col = patches[:, PATCH : PATCH + 1]
    lane = iota((size, G), 1)
    group = iota((size, 4 * PATCH_YZ), 1) // PATCH_YZ
    for a in range(PX):
        at = slice(a * size, (a + 1) * size)
        e_hi[at, :], e_lo[at, :] = split(x_basis(x_col + float(a), lane))
        p = jnp.concatenate([patches[:, a * PATCH_YZ : (a + 1) * PATCH_YZ]] * 4, axis=1)
        hi = p.astype(jnp.bfloat16).astype(jnp.float32)
        p_cat[at, :] = jnp.where(
            group == 3, 0.0, jnp.where(group == 1, p - hi, hi)
        ).astype(jnp.bfloat16)


def inverse_tables(cells, e_hi, e_lo):
    size = cells.shape[1]
    row = iota((G, size), 0)
    for a in range(PX):
        at = slice(a * size, (a + 1) * size)
        e_hi[:, at], e_lo[:, at] = split(x_basis(cells[0:1, :] + float(a), row))


def phases(base, chunk, ny, origin, cells):
    ky, kz = modes_at(base + iota((chunk, 1), 0), ny, origin)
    return sincos(ky.astype(jnp.float32) * cells[1:2, :] + kz.astype(jnp.float32) * cells[2:3, :])


def forward_chunk(base, chunk, ny, origin, phase, e, p_cat):
    ky, kz = modes_at(base + iota((chunk, 1), 0), ny, origin)
    lane = iota((1, 4 * PATCH_YZ), 1)
    cell = lane % PATCH_YZ
    group = lane // PATCH_YZ
    tables = jnp.concatenate(
        sincos(
            ky.astype(jnp.float32) * (cell // PZ).astype(jnp.float32)
            + kz.astype(jnp.float32) * (cell % PZ).astype(jnp.float32)
        ),
        axis=0,
    )
    hi = tables.astype(jnp.bfloat16).astype(jnp.float32)
    tables = jnp.where(group == 3, 0.0, jnp.where(group == 2, tables - hi, hi))
    f = lax.dot_general(
        tables.astype(jnp.bfloat16),
        p_cat,
        (((1,), (1,)), ((), ())),
        preferred_element_type=jnp.float32,
    )
    fc, fs = f[:chunk], f[chunk:]
    c, s = (jnp.concatenate([part] * PX, axis=1) for part in phase)
    m = jnp.concatenate([fc * c - fs * s, -(fc * s + fs * c)], axis=0)
    return dot3(split(m), e)


def apply_green(base, chunk, ny, origin, q):
    ky, kz = modes_at(base + iota((chunk, 1), 0), ny, origin)
    half = G // 2
    lane = iota((1, G), 1)
    unit = 2.0 * math.pi / G
    fx = jnp.where(lane > half, lane - half, lane).astype(jnp.float32) * unit
    fy, fz = folded(ky) * unit, folded(kz) * unit
    total = fx * fx + (fy * fy + fz * fz)
    divisor = jnp.where(total > 0, total, 1.0)
    green = jnp.where(
        total > 0, -4.0 * math.pi * jnp.exp(-total * (SCREEN * SCREEN)) / divisor, 0.0
    )
    green = green * jnp.where(lane % half == 0, 1.0, 2.0)
    return q * jnp.concatenate([green, green], axis=0)


def inverse_chunk(base, chunk, ny, origin, phase, e, h, acc):
    half = G // 2
    dx = slope(iota((1, half), 1))
    hx = jnp.concatenate([-(h[:, half:] * dx), h[:, :half] * dx], axis=1)
    lane = iota((1, 2 * chunk), 1)
    ky, kz = modes_at(base + lane % chunk, ny, origin)
    row = iota((PATCH_YZ, 1), 0)
    turn = jnp.where(lane < chunk, float(G // 4), 0.0)
    weight = jnp.where(
        (kz == 0) | (kz == half), 1.0, jnp.where(kz < half, 2.0, 0.0)
    ) * (1.0 / float(G * G * G))
    angle = ky.astype(jnp.float32) * (row // PZ).astype(jnp.float32) + kz.astype(jnp.float32) * (
        row % PZ
    ).astype(jnp.float32)
    slopes = sincos(angle - turn)[0] * weight
    c, s = (jnp.concatenate([part] * PX, axis=1) for part in phase)

    def add(source, at, table):
        p = dot3(split(source), e)
        real, imag = p[:chunk], p[chunk:]
        turned = split(jnp.concatenate([real * c - imag * s, real * s + imag * c], axis=0))
        hi, lo = split(table)
        rows = table.shape[0]
        dot = functools.partial(jnp.dot, preferred_element_type=jnp.float32)
        both = dot(jnp.concatenate([hi, lo], axis=0), turned[0])
        acc[at, :] += both[:rows] + (both[rows:] + dot(hi, turned[1]))

    cosine = sincos(angle - turn + float(G // 4))[0] * weight
    add(hx, slice(0, PATCH_YZ), cosine)
    add(
        h,
        slice(PATCH_YZ, 3 * PATCH_YZ),
        jnp.concatenate([slopes * slope(ky), slopes * slope(kz)], axis=0),
    )


def write_field(acc, out):
    size = out.shape[0]
    for f in range(3):
        for a in range(PX):
            block = acc[f * PATCH_YZ : (f + 1) * PATCH_YZ, a * size : (a + 1) * size]
            col = f * PATCH + a * PATCH_YZ
            out[:, col : col + PATCH_YZ] = block.T


def whole_kernel(ny, chunk, modes, origin, patches, out, e_hi, e_lo, p_cat, i_hi, i_lo, acc):
    cells = patches[:, PATCH:].T
    forward_tables(patches, e_hi, e_lo, p_cat)
    inverse_tables(cells, i_hi, i_lo)
    acc[...] = jnp.zeros_like(acc)

    def body(i, carry):
        base = i * chunk
        phase = phases(base, chunk, ny, origin, cells)
        q = forward_chunk(base, chunk, ny, origin, phase, (e_hi[...], e_lo[...]), p_cat[...])
        h = apply_green(base, chunk, ny, origin, q)
        inverse_chunk(base, chunk, ny, origin, phase, (i_hi[...], i_lo[...]), h, acc)
        return carry

    lax.fori_loop(0, modes // chunk, body, 0)
    write_field(acc, out)


def forward_kernel(ny, chunk, origin, patches, out, e_hi, e_lo, p_cat):
    step = pl.program_id(0)
    cells = patches[:, PATCH:].T
    forward_tables(patches, e_hi, e_lo, p_cat)

    @pl.when(step == 0)
    def _():
        out[...] = jnp.zeros_like(out)

    def body(i, carry):
        base = i * chunk
        at = pl.ds(pl.multiple_of(2 * base, 8), 2 * chunk)
        phase = phases(base, chunk, ny, origin, cells)
        out[at, :] += forward_chunk(
            base, chunk, ny, origin, phase, (e_hi[...], e_lo[...]), p_cat[...]
        )

        @pl.when(step == pl.num_programs(0) - 1)
        def _():
            out[at, :] = apply_green(base, chunk, ny, origin, out[at, :])

        return carry

    lax.fori_loop(0, out.shape[0] // (2 * chunk), body, 0)


def inverse_kernel(ny, chunk, origin, spectrum, patches, out, i_hi, i_lo, acc):
    cells = patches[:, PATCH:].T
    inverse_tables(cells, i_hi, i_lo)
    acc[...] = jnp.zeros_like(acc)

    def body(i, carry):
        base = i * chunk
        at = pl.ds(pl.multiple_of(2 * base, 8), 2 * chunk)
        phase = phases(base, chunk, ny, origin, cells)
        inverse_chunk(
            base, chunk, ny, origin, phase, (i_hi[...], i_lo[...]), spectrum[at, :], acc
        )
        return carry

    lax.fori_loop(0, spectrum.shape[0] // (2 * chunk), body, 0)
    write_field(acc, out)


def pair_kernel(leaves, slots, exports, notes, books, out):
    out[...] = jnp.zeros_like(out)

    def job(rank, target, pick):
        tgt = books[0, target]
        total = [0.0, 0.0, 0.0]
        for k in range(2):
            source = notes[rank, target, 3 + k]
            src = books[rank, source]
            cols = src.T
            members = src.shape[1]
            d = []
            for c in range(3):
                apart = (notes[rank, source, c] - notes[0, target, c]).astype(jnp.float32)
                wraps = (apart > 0.5 * G).astype(jnp.int32) - (apart <= -0.5 * G).astype(jnp.int32)
                col = cols[:, c : c + 1] - float(G) * wraps.astype(jnp.float32)
                d.append(jnp.broadcast_to(col, (members, members)) - tgt[c : c + 1, :])
            squared = d[0] * d[0] + d[1] * d[1] + d[2] * d[2]
            r = squared * lax.rsqrt(jnp.maximum(squared, 1e-30))
            t = 1.0 / (1.0 + 0.5 * r)
            poly = ERFCX[-1] * t + ERFCX[-2]
            for coefficient in ERFCX[-3::-1]:
                poly = poly * t + coefficient
            screened = jnp.exp(-squared) * (poly * t + (2.0 / math.sqrt(math.pi)) * r)
            inv = lax.rsqrt(squared + SOFTEN * SOFTEN)
            w = cols[:, 3:4] * screened * (inv * inv * inv)
            for c in range(3):
                total[c] = total[c] + jnp.sum(w * d[c], axis=0, keepdims=True)
        out[target, 0:3, :] += jnp.concatenate(total, axis=0) * pick

    def own(n, carry):
        job(0, n, 1.0)
        return carry

    def guest(j, carry):
        face = j // slots
        leaf = exports[face, j % slots]
        job(face + 1, jnp.minimum(leaf, leaves - 1), (leaf < leaves).astype(jnp.float32))
        return carry

    lax.fori_loop(0, leaves, own, 0)
    lax.fori_loop(0, 4 * slots, guest, 0)


def sample_kernel(field, fraction, short, out):
    leaves = field.shape[0]
    members = fraction.shape[1] // leaves
    for n in range(leaves):
        at = slice(n * members, (n + 1) * members)
        w = split(leaf_weights(fraction[:, at]))
        values = jnp.concatenate(
            [field[n : n + 1, f * PATCH : (f + 1) * PATCH] for f in range(3)], axis=0
        )
        out[:, at] = dot3(split(values), w) + short[n, 0:3, :]


def local(fraction, masses, leaf_cell, exports, tile_lists):
    leaves = leaf_cell.shape[1]
    members = masses.shape[0] // leaves
    slots = exports.shape[1]
    n_wide, n_narrow = lax.axis_size("wide"), lax.axis_size("narrow")
    total = leaves * n_wide * n_narrow
    f32 = jnp.float32

    packed, book = pl.pallas_call(
        pack_kernel,
        out_shape=(
            jax.ShapeDtypeStruct((leaves, 2 * PATCH), f32),
            jax.ShapeDtypeStruct((leaves, 8, members), f32),
        ),
        in_specs=[SMEM, SMEM, VMEM, VMEM],
        out_specs=(VMEM, VMEM),
        name="pack",
    )(leaf_cell, tile_lists, fraction, masses.reshape(1, -1))
    copies = n_wide - 1 + n_narrow - 1
    gathered, books = pl.pallas_call(
        gather_kernel,
        out_shape=(
            jax.ShapeDtypeStruct((n_wide, n_narrow, leaves, 2 * PATCH), f32),
            jax.ShapeDtypeStruct((5, leaves, 8, members), f32),
        ),
        in_specs=[VMEM, VMEM],
        out_specs=(VMEM, VMEM),
        scratch_shapes=[
            pltpu.SemaphoreType.DMA((2,)),
            pltpu.SemaphoreType.DMA((copies + 4,)),
            pltpu.SemaphoreType.DMA((copies + 4,)),
        ],
        compiler_params=pltpu.CompilerParams(collective_id=0, has_side_effects=True),
        name="gather",
    )(packed, book)
    gathered = gathered.reshape(total, 2 * PATCH)
    notes = books[:, :, 4, 0:5].astype(jnp.int32)
    short = pl.pallas_call(
        functools.partial(pair_kernel, leaves, slots),
        out_shape=jax.ShapeDtypeStruct((leaves, 8, members), f32),
        in_specs=[SMEM, SMEM, VMEM],
        out_specs=VMEM,
        name="pairs",
    )(exports, notes, books)

    nz = -(-(G // 2 + 1) // n_narrow)
    ny = G // n_wide
    modes = nz * ny
    parts = next(p for p in range(1, modes + 1) if nz % p == 0 and modes // p <= 384)
    chunk = modes // parts
    origin = jnp.stack([lax.axis_index("narrow") * nz, lax.axis_index("wide") * ny]).astype(
        jnp.int32
    )
    size = min(total, 256)
    blocks = total // size
    params = pltpu.CompilerParams(vmem_limit_bytes=56 * 2**20)
    forward_scratch = [
        pltpu.VMEM((PX * size, G), jnp.bfloat16),
        pltpu.VMEM((PX * size, G), jnp.bfloat16),
        pltpu.VMEM((PX * size, 4 * PATCH_YZ), jnp.bfloat16),
    ]
    inverse_scratch = [
        pltpu.VMEM((G, PX * size), jnp.bfloat16),
        pltpu.VMEM((G, PX * size), jnp.bfloat16),
        pltpu.VMEM((3 * PATCH_YZ, PX * size), f32),
    ]
    field_shape = jax.ShapeDtypeStruct((total, 3 * PATCH), f32)
    leaf_rows = pl.BlockSpec((size, 2 * PATCH), lambda i: (i, 0))
    spectrum_all = pl.BlockSpec((2 * modes, G), lambda i: (0, 0))
    if blocks == 1:
        partial = pl.pallas_call(
            functools.partial(whole_kernel, ny, chunk, modes),
            out_shape=field_shape,
            in_specs=[SMEM, VMEM],
            out_specs=VMEM,
            scratch_shapes=forward_scratch + inverse_scratch,
            compiler_params=params,
            name="transform",
        )(origin, gathered)
    else:
        spectrum = pl.pallas_call(
            functools.partial(forward_kernel, ny, chunk),
            grid=(blocks,),
            out_shape=jax.ShapeDtypeStruct((2 * modes, G), f32),
            in_specs=[SMEM, leaf_rows],
            out_specs=spectrum_all,
            scratch_shapes=forward_scratch,
            compiler_params=params,
            name="forward",
        )(origin, gathered)
        partial = pl.pallas_call(
            functools.partial(inverse_kernel, ny, chunk),
            grid=(blocks,),
            out_shape=field_shape,
            in_specs=[SMEM, spectrum_all, leaf_rows],
            out_specs=pl.BlockSpec((size, 3 * PATCH), lambda i: (i, 0)),
            scratch_shapes=inverse_scratch,
            compiler_params=params,
            name="inverse",
        )(origin, spectrum, gathered)
    block = (leaves, 3 * PATCH)
    field = pl.pallas_call(
        scatter_kernel,
        out_shape=jax.ShapeDtypeStruct(block, f32),
        in_specs=[VMEM],
        out_specs=VMEM,
        scratch_shapes=[
            pltpu.VMEM((n_wide - 1, n_narrow) + block, f32),
            pltpu.VMEM((n_narrow,) + block, f32),
            pltpu.VMEM((n_narrow - 1,) + block, f32),
            pltpu.SemaphoreType.DMA((copies,)),
            pltpu.SemaphoreType.DMA((copies,)),
        ],
        compiler_params=pltpu.CompilerParams(collective_id=1, has_side_effects=True),
        name="scatter",
    )(partial.reshape((n_wide, n_narrow) + block))
    return pl.pallas_call(
        sample_kernel,
        out_shape=jax.ShapeDtypeStruct((3, leaves * members), f32),
        in_specs=[VMEM, VMEM, VMEM],
        out_specs=VMEM,
        name="sample",
    )(field, fraction, short)


def solution(mesh):
    placed = (
        P(None, ("wide", "narrow")),
        P(("wide", "narrow")),
        P(None, ("wide", "narrow")),
        P(None, ("wide", "narrow")),
        P(None, ("wide", "narrow")),
    )
    return jax.shard_map(
        local, mesh=mesh, in_specs=placed, out_specs=P(None, ("wide", "narrow")), check_vma=False
    )
```

```python
import functools
import math

import jax
import jax.numpy as jnp
from jax import lax
from jax.experimental import pallas as pl
from jax.experimental.pallas import tpu as pltpu
from jax.sharding import PartitionSpec as P

G = 256
PX = 2
PY = 4
PZ = 16
PATCH_YZ = PY * PZ
PATCH = PX * PATCH_YZ
SCREEN = 0.5
SOFTEN = 0.5
ERFCX = (
    0.2820947416810428,
    0.28210427504184366,
    0.24651391069954823,
    0.18039116519942175,
    0.058372405908860704,
    0.0792320361696661,
    -0.1983246779625943,
    0.030722780905291756,
    0.06437369661731697,
    -0.025480486181070308,
)
VMEM = pl.BlockSpec(memory_space=pltpu.VMEM)
SMEM = pl.BlockSpec(memory_space=pltpu.SMEM)


def iota(shape, dim):
    return lax.broadcasted_iota(jnp.int32, shape, dim)


def sincos(count):
    quarters = count * (4.0 / G)
    near = jnp.floor(quarters + 0.5)
    z = (quarters - near) * (math.pi / 2)
    q = near.astype(jnp.int32)
    zz = z * z
    c = 1.0 + zz * (-0.5 + zz * (1.0 / 24 + zz * (-1.0 / 720 + zz * (1.0 / 40320))))
    s = z * (1.0 + zz * (-1.0 / 6 + zz * (1.0 / 120 + zz * (-1.0 / 5040))))
    swap = (q & 1) == 1
    cosine = jnp.where(swap, s, c)
    sine = jnp.where(swap, c, s)
    cosine = jnp.where(((q + 1) & 2) == 2, -cosine, cosine)
    sine = jnp.where((q & 2) == 2, -sine, sine)
    return cosine, sine


def split(x):
    hi = x.astype(jnp.bfloat16)
    return hi, (x - hi.astype(jnp.float32)).astype(jnp.bfloat16)


def dot3(left, right, dims=((1,), (0,))):
    dims = (dims, ((), ()))
    dot = functools.partial(
        lax.dot_general, dimension_numbers=dims, preferred_element_type=jnp.float32
    )
    return dot(left[0], right[0]) + (dot(left[0], right[1]) + dot(left[1], right[0]))


def folded(wave):
    return jnp.where(wave > G // 2, wave - G, wave).astype(jnp.float32)


def slope(wave):
    w = wave.astype(jnp.float32)
    return (8.0 * sincos(w)[1] - sincos(2.0 * w)[1]) * (1.0 / 6.0)


def leaf_weights(u):
    members = u.shape[1]
    row = iota((PATCH, members), 0)
    cells = (row // PATCH_YZ, row // PZ % PY, row % PZ)
    product = None
    for c, extent in enumerate((PX, PY, PZ)):
        centre = cells[c].astype(jnp.float32) + 0.5
        coordinate = 0.5 + u[c : c + 1] * (extent - 1.0)
        w = jnp.maximum(0.0, 1.0 - jnp.abs(coordinate - centre))
        product = w if product is None else product * w
    return product


def pack_kernel(leaf_cell, tile_lists, fraction, masses, packed, book):
    leaves = packed.shape[0]
    members = masses.shape[1] // leaves
    lane = iota((1, members), 1)
    for n in range(leaves):
        at = slice(n * members, (n + 1) * members)
        u = fraction[:, at]
        m = masses[:, at]
        w = leaf_weights(u)
        full = jnp.broadcast_to(m, (8, members))
        packed[n : n + 1, 0:PATCH] = dot3(split(full), split(w), ((1,), (1,)))[0:1, :]
        cell = [leaf_cell[c, n].astype(jnp.float32) for c in range(3)]
        note = jnp.zeros((1, members), jnp.float32)
        for c in range(3):
            note = jnp.where(lane == c, cell[c], note)
        packed[n : n + 1, PATCH:] = note[:, 0:PATCH]
        for k in range(2):
            note = jnp.where(lane == 3 + k, tile_lists[k, n].astype(jnp.float32), note)
        for c, extent in enumerate((PX, PY, PZ)):
            book[n, c : c + 1, :] = cell[c] + (u[c : c + 1] * (extent - 1.0) + 0.5)
        book[n, 3:4, :] = m
        book[n, 4:5, :] = note
        book[n, 5:8, :] = jnp.zeros((3, members), jnp.float32)


def peers_of(axis):
    count = lax.axis_size(axis)
    me = lax.axis_index(axis)
    return [(axis, s, lax.rem(me + s, count), lax.rem(me + count - s, count)) for s in range(1, count)]


def greet(groups):
    barrier = pltpu.get_barrier_semaphore()
    for axis, _, ahead, _ in groups:
        pl.semaphore_signal(
            barrier, inc=1, device_id={axis: ahead}, device_id_type=pl.DeviceIdType.MESH
        )
    pl.semaphore_wait(barrier, len(groups))


def remote(src, dst, send, recv, axis, to):
    return pltpu.make_async_remote_copy(
        src_ref=src,
        dst_ref=dst,
        send_sem=send,
        recv_sem=recv,
        device_id={axis: to},
        device_id_type=pl.DeviceIdType.MESH,
    )


def gather_kernel(packed, book, out, books, own, sends, recvs):
    wide, narrow = peers_of("wide"), peers_of("narrow")
    w, v = lax.axis_index("wide"), lax.axis_index("narrow")
    keep = [
        pltpu.make_async_copy(packed, out.at[w, v], own.at[0]),
        pltpu.make_async_copy(book, books.at[0], own.at[1]),
    ]
    for copy in keep:
        copy.start()
    greet(wide + narrow)
    at = 0
    first = []
    for axis, s, ahead, _ in narrow:
        first.append(remote(packed, out.at[w, v], sends.at[at], recvs.at[at], axis, ahead))
        at += 1
    for copy in first:
        copy.start()
    near = []
    for slot, (axis, to) in enumerate(
        (
            ("wide", wide[-1][2]),
            ("wide", wide[0][2]),
            ("narrow", narrow[-1][2]),
            ("narrow", narrow[0][2]),
        )
    ):
        near.append(remote(book, books.at[slot + 1], sends.at[at], recvs.at[at], axis, to))
        at += 1
    for copy in keep:
        copy.wait()
    for copy, (axis, s, _, behind) in zip(first, narrow):
        remote(
            packed, out.at[w, behind], sends.at[s - 1], recvs.at[s - 1], axis, behind
        ).wait_recv()
    second = []
    base = at
    for axis, s, ahead, _ in wide:
        second.append(remote(out.at[w], out.at[w], sends.at[at], recvs.at[at], axis, ahead))
        at += 1
    for copy in second + near:
        copy.start()
    for axis, s, _, behind in wide:
        i = base + s - 1
        remote(out.at[w], out.at[behind], sends.at[i], recvs.at[i], axis, behind).wait_recv()
    for copy in near:
        copy.wait_recv()
    for copy in first + second + near:
        copy.wait_send()


def modes_at(index, ny, origin):
    return origin[1] + index % ny, origin[0] + index // ny


def x_basis(x, lane):
    half = G // 2
    wave = jnp.where(lane > half, lane - half, lane).astype(jnp.float32)
    turn = jnp.where(lane > half, float(G // 4), 0.0)
    return sincos(x * wave - turn)[0]


def forward_tables(patches, e_hi, e_lo, p_cat):
    size = patches.shape[0]
    x_col = patches[:, PATCH : PATCH + 1]
    lane = iota((size, G), 1)
    group = iota((size, 4 * PATCH_YZ), 1) // PATCH_YZ
    for a in range(PX):
        at = slice(a * size, (a + 1) * size)
        e_hi[at, :], e_lo[at, :] = split(x_basis(x_col + float(a), lane))
        p = jnp.concatenate([patches[:, a * PATCH_YZ : (a + 1) * PATCH_YZ]] * 4, axis=1)
        hi = p.astype(jnp.bfloat16).astype(jnp.float32)
        p_cat[at, :] = jnp.where(
            group == 3, 0.0, jnp.where(group == 1, p - hi, hi)
        ).astype(jnp.bfloat16)


def inverse_tables(cells, e_hi, e_lo):
    size = cells.shape[1]
    row = iota((G, size), 0)
    for a in range(PX):
        at = slice(a * size, (a + 1) * size)
        e_hi[:, at], e_lo[:, at] = split(x_basis(cells[0:1, :] + float(a), row))


def phases(base, chunk, ny, origin, cells):
    ky, kz = modes_at(base + iota((chunk, 1), 0), ny, origin)
    return sincos(ky.astype(jnp.float32) * cells[1:2, :] + kz.astype(jnp.float32) * cells[2:3, :])


def forward_chunk(base, chunk, ny, origin, phase, e, p_cat):
    ky, kz = modes_at(base + iota((chunk, 1), 0), ny, origin)
    lane = iota((1, 4 * PATCH_YZ), 1)
    cell = lane % PATCH_YZ
    group = lane // PATCH_YZ
    tables = jnp.concatenate(
        sincos(
            ky.astype(jnp.float32) * (cell // PZ).astype(jnp.float32)
            + kz.astype(jnp.float32) * (cell % PZ).astype(jnp.float32)
        ),
        axis=0,
    )
    hi = tables.astype(jnp.bfloat16).astype(jnp.float32)
    tables = jnp.where(group == 3, 0.0, jnp.where(group == 2, tables - hi, hi))
    f = lax.dot_general(
        tables.astype(jnp.bfloat16),
        p_cat,
        (((1,), (1,)), ((), ())),
        preferred_element_type=jnp.float32,
    )
    fc, fs = f[:chunk], f[chunk:]
    c, s = (jnp.concatenate([part] * PX, axis=1) for part in phase)
    m = jnp.concatenate([fc * c - fs * s, -(fc * s + fs * c)], axis=0)
    return dot3(split(m), e)


def apply_green(base, chunk, ny, origin, q):
    ky, kz = modes_at(base + iota((chunk, 1), 0), ny, origin)
    half = G // 2
    lane = iota((1, G), 1)
    unit = 2.0 * math.pi / G
    fx = jnp.where(lane > half, lane - half, lane).astype(jnp.float32) * unit
    fy, fz = folded(ky) * unit, folded(kz) * unit
    total = fx * fx + (fy * fy + fz * fz)
    divisor = jnp.where(total > 0, total, 1.0)
    green = jnp.where(
        total > 0, -4.0 * math.pi * jnp.exp(-total * (SCREEN * SCREEN)) / divisor, 0.0
    )
    green = green * jnp.where(lane % half == 0, 1.0, 2.0)
    return q * jnp.concatenate([green, green], axis=0)


def inverse_chunk(base, chunk, ny, origin, phase, e, h, acc):
    half = G // 2
    dx = slope(iota((1, half), 1))
    hx = jnp.concatenate([-(h[:, half:] * dx), h[:, :half] * dx], axis=1)
    lane = iota((1, 2 * chunk), 1)
    ky, kz = modes_at(base + lane % chunk, ny, origin)
    row = iota((PATCH_YZ, 1), 0)
    turn = jnp.where(lane < chunk, float(G // 4), 0.0)
    weight = jnp.where(
        (kz == 0) | (kz == half), 1.0, jnp.where(kz < half, 2.0, 0.0)
    ) * (1.0 / float(G * G * G))
    angle = ky.astype(jnp.float32) * (row // PZ).astype(jnp.float32) + kz.astype(jnp.float32) * (
        row % PZ
    ).astype(jnp.float32)
    slopes = sincos(angle - turn)[0] * weight
    c, s = (jnp.concatenate([part] * PX, axis=1) for part in phase)

    def add(source, at, table):
        p = dot3(split(source), e)
        real, imag = p[:chunk], p[chunk:]
        turned = split(jnp.concatenate([real * c - imag * s, real * s + imag * c], axis=0))
        hi, lo = split(table)
        rows = table.shape[0]
        dot = functools.partial(jnp.dot, preferred_element_type=jnp.float32)
        both = dot(jnp.concatenate([hi, lo], axis=0), turned[0])
        acc[at, :] += both[:rows] + (both[rows:] + dot(hi, turned[1]))

    cosine = sincos(angle - turn + float(G // 4))[0] * weight
    add(hx, slice(0, PATCH_YZ), cosine)
    add(
        h,
        slice(PATCH_YZ, 3 * PATCH_YZ),
        jnp.concatenate([slopes * slope(ky), slopes * slope(kz)], axis=0),
    )


def write_field(acc, out):
    size = out.shape[0]
    for f in range(3):
        for a in range(PX):
            block = acc[f * PATCH_YZ : (f + 1) * PATCH_YZ, a * size : (a + 1) * size]
            col = f * PATCH + a * PATCH_YZ
            out[:, col : col + PATCH_YZ] = block.T


def whole_kernel(ny, chunk, modes, origin, patches, out, e_hi, e_lo, p_cat, i_hi, i_lo, acc):
    cells = patches[:, PATCH:].T
    forward_tables(patches, e_hi, e_lo, p_cat)
    inverse_tables(cells, i_hi, i_lo)
    acc[...] = jnp.zeros_like(acc)

    def body(i, carry):
        base = i * chunk
        phase = phases(base, chunk, ny, origin, cells)
        q = forward_chunk(base, chunk, ny, origin, phase, (e_hi[...], e_lo[...]), p_cat[...])
        h = apply_green(base, chunk, ny, origin, q)
        inverse_chunk(base, chunk, ny, origin, phase, (i_hi[...], i_lo[...]), h, acc)
        return carry

    lax.fori_loop(0, modes // chunk, body, 0)
    write_field(acc, out)


def forward_kernel(ny, chunk, origin, patches, out, e_hi, e_lo, p_cat):
    step = pl.program_id(0)
    cells = patches[:, PATCH:].T
    forward_tables(patches, e_hi, e_lo, p_cat)

    @pl.when(step == 0)
    def _():
        out[...] = jnp.zeros_like(out)

    def body(i, carry):
        base = i * chunk
        at = pl.ds(pl.multiple_of(2 * base, 8), 2 * chunk)
        phase = phases(base, chunk, ny, origin, cells)
        out[at, :] += forward_chunk(
            base, chunk, ny, origin, phase, (e_hi[...], e_lo[...]), p_cat[...]
        )

        @pl.when(step == pl.num_programs(0) - 1)
        def _():
            out[at, :] = apply_green(base, chunk, ny, origin, out[at, :])

        return carry

    lax.fori_loop(0, out.shape[0] // (2 * chunk), body, 0)


def inverse_kernel(ny, chunk, origin, spectrum, patches, out, i_hi, i_lo, acc):
    cells = patches[:, PATCH:].T
    inverse_tables(cells, i_hi, i_lo)
    acc[...] = jnp.zeros_like(acc)

    def body(i, carry):
        base = i * chunk
        at = pl.ds(pl.multiple_of(2 * base, 8), 2 * chunk)
        phase = phases(base, chunk, ny, origin, cells)
        inverse_chunk(
            base, chunk, ny, origin, phase, (i_hi[...], i_lo[...]), spectrum[at, :], acc
        )
        return carry

    lax.fori_loop(0, spectrum.shape[0] // (2 * chunk), body, 0)
    write_field(acc, out)


def pair_jobs(leaves, slots, exports, notes, books, forces):
    def job(j, rank, target):
        tgt = books[0, target]
        total = [0.0, 0.0, 0.0]
        for k in range(2):
            source = notes[rank, target, 3 + k]
            src = books[rank, source]
            cols = src.T
            members = src.shape[1]
            d = []
            for c in range(3):
                apart = (notes[rank, source, c] - notes[0, target, c]).astype(jnp.float32)
                wraps = (apart > 0.5 * G).astype(jnp.int32) - (apart <= -0.5 * G).astype(jnp.int32)
                col = cols[:, c : c + 1] - float(G) * wraps.astype(jnp.float32)
                d.append(jnp.broadcast_to(col, (members, members)) - tgt[c : c + 1, :])
            squared = d[0] * d[0] + d[1] * d[1] + d[2] * d[2]
            r = squared * lax.rsqrt(jnp.maximum(squared, 1e-30))
            t = 1.0 / (1.0 + 0.5 * r)
            poly = ERFCX[-1] * t + ERFCX[-2]
            for coefficient in ERFCX[-3::-1]:
                poly = poly * t + coefficient
            screened = jnp.exp(-squared) * (poly * t + (2.0 / math.sqrt(math.pi)) * r)
            inv = lax.rsqrt(squared + SOFTEN * SOFTEN)
            w = cols[:, 3:4] * screened * (inv * inv * inv)
            for c in range(3):
                total[c] = total[c] + jnp.sum(w * d[c], axis=0, keepdims=True)
        forces[j] = jnp.concatenate(total + [jnp.zeros((5,) + total[0].shape[1:], jnp.float32)], axis=0)

    def own(n, carry):
        job(n, 0, n)
        return carry

    def guest(j, carry):
        face = j // slots
        job(leaves + j, face + 1, jnp.minimum(exports[face, j % slots], leaves - 1))
        return carry

    lax.fori_loop(0, leaves, own, 0)
    lax.fori_loop(0, 4 * slots, guest, 0)


def finish_kernel(
    exports, notes, books, fraction, partial, out, landed, mine, near, forces, w_hi, w_lo, sends, recvs
):
    wide, narrow = peers_of("wide"), peers_of("narrow")
    w, v = lax.axis_index("wide"), lax.axis_index("narrow")
    leaves = mine.shape[1]
    slots = exports.shape[1]
    members = fraction.shape[1] // leaves
    greet(wide + narrow)
    at = 0
    first = []
    for axis, s, ahead, _ in wide:
        first.append(
            remote(partial.at[ahead], landed.at[s - 1], sends.at[at], recvs.at[at], axis, ahead)
        )
        at += 1
    for copy in first:
        copy.start()
    pair_jobs(leaves, slots, exports, notes, books, forces)
    for copy in first:
        copy.wait_recv()
    total = partial[w]
    for s in range(len(wide)):
        total = total + landed[s]
    mine[...] = total
    second = []
    for axis, s, ahead, _ in narrow:
        second.append(
            remote(mine.at[ahead], near.at[s - 1], sends.at[at], recvs.at[at], axis, ahead)
        )
        at += 1
    for copy in second:
        copy.start()
    short = []
    for n in range(leaves):
        w_hi[n], w_lo[n] = split(leaf_weights(fraction[:, n * members : (n + 1) * members]))
        force = forces[n]
        for j in range(4 * slots):
            mine_too = jnp.where(exports[j // slots, j % slots] == n, 1.0, 0.0)
            force = force + forces[leaves + j] * mine_too
        short.append(force)
    for copy in second:
        copy.wait_recv()
    field = mine[v]
    for s in range(len(narrow)):
        field = field + near[s]
    for n in range(leaves):
        values = jnp.concatenate(
            [field[n : n + 1, f * PATCH : (f + 1) * PATCH] for f in range(3)], axis=0
        )
        got = dot3(split(values), (w_hi[n], w_lo[n]))
        out[:, n * members : (n + 1) * members] = got + short[n][0:3, :]
    for copy in first + second:
        copy.wait_send()


def local(fraction, masses, leaf_cell, exports, tile_lists):
    leaves = leaf_cell.shape[1]
    members = masses.shape[0] // leaves
    slots = exports.shape[1]
    n_wide, n_narrow = lax.axis_size("wide"), lax.axis_size("narrow")
    total = leaves * n_wide * n_narrow
    f32 = jnp.float32

    packed, book = pl.pallas_call(
        pack_kernel,
        out_shape=(
            jax.ShapeDtypeStruct((leaves, 2 * PATCH), f32),
            jax.ShapeDtypeStruct((leaves, 8, members), f32),
        ),
        in_specs=[SMEM, SMEM, VMEM, VMEM],
        out_specs=(VMEM, VMEM),
        name="pack",
    )(leaf_cell, tile_lists, fraction, masses.reshape(1, -1))
    copies = n_wide - 1 + n_narrow - 1
    gathered, books = pl.pallas_call(
        gather_kernel,
        out_shape=(
            jax.ShapeDtypeStruct((n_wide, n_narrow, leaves, 2 * PATCH), f32),
            jax.ShapeDtypeStruct((5, leaves, 8, members), f32),
        ),
        in_specs=[VMEM, VMEM],
        out_specs=(VMEM, VMEM),
        scratch_shapes=[
            pltpu.SemaphoreType.DMA((2,)),
            pltpu.SemaphoreType.DMA((copies + 4,)),
            pltpu.SemaphoreType.DMA((copies + 4,)),
        ],
        compiler_params=pltpu.CompilerParams(collective_id=0, has_side_effects=True),
        name="gather",
    )(packed, book)
    gathered = gathered.reshape(total, 2 * PATCH)
    notes = books[:, :, 4, 0:5].astype(jnp.int32)
    nz = -(-(G // 2 + 1) // n_narrow)
    ny = G // n_wide
    modes = nz * ny
    parts = next(p for p in range(1, modes + 1) if nz % p == 0 and modes // p <= 384)
    chunk = modes // parts
    origin = jnp.stack([lax.axis_index("narrow") * nz, lax.axis_index("wide") * ny]).astype(
        jnp.int32
    )
    size = min(total, 256)
    blocks = total // size
    params = pltpu.CompilerParams(vmem_limit_bytes=56 * 2**20)
    forward_scratch = [
        pltpu.VMEM((PX * size, G), jnp.bfloat16),
        pltpu.VMEM((PX * size, G), jnp.bfloat16),
        pltpu.VMEM((PX * size, 4 * PATCH_YZ), jnp.bfloat16),
    ]
    inverse_scratch = [
        pltpu.VMEM((G, PX * size), jnp.bfloat16),
        pltpu.VMEM((G, PX * size), jnp.bfloat16),
        pltpu.VMEM((3 * PATCH_YZ, PX * size), f32),
    ]
    field_shape = jax.ShapeDtypeStruct((total, 3 * PATCH), f32)
    leaf_rows = pl.BlockSpec((size, 2 * PATCH), lambda i: (i, 0))
    spectrum_all = pl.BlockSpec((2 * modes, G), lambda i: (0, 0))
    if blocks == 1:
        partial = pl.pallas_call(
            functools.partial(whole_kernel, ny, chunk, modes),
            out_shape=field_shape,
            in_specs=[SMEM, VMEM],
            out_specs=VMEM,
            scratch_shapes=forward_scratch + inverse_scratch,
            compiler_params=params,
            name="transform",
        )(origin, gathered)
    else:
        spectrum = pl.pallas_call(
            functools.partial(forward_kernel, ny, chunk),
            grid=(blocks,),
            out_shape=jax.ShapeDtypeStruct((2 * modes, G), f32),
            in_specs=[SMEM, leaf_rows],
            out_specs=spectrum_all,
            scratch_shapes=forward_scratch,
            compiler_params=params,
            name="forward",
        )(origin, gathered)
        partial = pl.pallas_call(
            functools.partial(inverse_kernel, ny, chunk),
            grid=(blocks,),
            out_shape=field_shape,
            in_specs=[SMEM, spectrum_all, leaf_rows],
            out_specs=pl.BlockSpec((size, 3 * PATCH), lambda i: (i, 0)),
            scratch_shapes=inverse_scratch,
            compiler_params=params,
            name="inverse",
        )(origin, spectrum, gathered)
    block = (leaves, 3 * PATCH)
    return pl.pallas_call(
        finish_kernel,
        out_shape=jax.ShapeDtypeStruct((3, leaves * members), f32),
        in_specs=[SMEM, SMEM, VMEM, VMEM, VMEM],
        out_specs=VMEM,
        scratch_shapes=[
            pltpu.VMEM((n_wide - 1, n_narrow) + block, f32),
            pltpu.VMEM((n_narrow,) + block, f32),
            pltpu.VMEM((n_narrow - 1,) + block, f32),
            pltpu.VMEM((leaves + 4 * slots, 8, members), f32),
            pltpu.VMEM((leaves, PATCH, members), jnp.bfloat16),
            pltpu.VMEM((leaves, PATCH, members), jnp.bfloat16),
            pltpu.SemaphoreType.DMA((copies,)),
            pltpu.SemaphoreType.DMA((copies,)),
        ],
        compiler_params=pltpu.CompilerParams(collective_id=1, has_side_effects=True),
        name="finish",
    )(exports, notes, books, fraction, partial.reshape((n_wide, n_narrow) + block))


def solution(mesh):
    placed = (
        P(None, ("wide", "narrow")),
        P(("wide", "narrow")),
        P(None, ("wide", "narrow")),
        P(None, ("wide", "narrow")),
        P(None, ("wide", "narrow")),
    )
    return jax.shard_map(
        local, mesh=mesh, in_specs=placed, out_specs=P(None, ("wide", "narrow")), check_vma=False
    )
```

```python
import functools
import math

import jax
import jax.numpy as jnp
from jax import lax
from jax.experimental import pallas as pl
from jax.experimental.pallas import tpu as pltpu
from jax.sharding import PartitionSpec as P

G = 256
PX = 2
PY = 4
PZ = 16
PATCH_YZ = PY * PZ
PATCH = PX * PATCH_YZ
SCREEN = 0.5
SOFTEN = 0.5
ERFCX = (
    0.2820947416810428,
    0.28210427504184366,
    0.24651391069954823,
    0.18039116519942175,
    0.058372405908860704,
    0.0792320361696661,
    -0.1983246779625943,
    0.030722780905291756,
    0.06437369661731697,
    -0.025480486181070308,
)
VMEM = pl.BlockSpec(memory_space=pltpu.VMEM)
SMEM = pl.BlockSpec(memory_space=pltpu.SMEM)


def iota(shape, dim):
    return lax.broadcasted_iota(jnp.int32, shape, dim)


def sincos(count):
    quarters = count * (4.0 / G)
    near = jnp.floor(quarters + 0.5)
    z = (quarters - near) * (math.pi / 2)
    q = near.astype(jnp.int32)
    zz = z * z
    c = 1.0 + zz * (-0.5 + zz * (1.0 / 24 + zz * (-1.0 / 720 + zz * (1.0 / 40320))))
    s = z * (1.0 + zz * (-1.0 / 6 + zz * (1.0 / 120 + zz * (-1.0 / 5040))))
    swap = (q & 1) == 1
    cosine = jnp.where(swap, s, c)
    sine = jnp.where(swap, c, s)
    cosine = jnp.where(((q + 1) & 2) == 2, -cosine, cosine)
    sine = jnp.where((q & 2) == 2, -sine, sine)
    return cosine, sine


def split(x):
    hi = x.astype(jnp.bfloat16)
    return hi, (x - hi.astype(jnp.float32)).astype(jnp.bfloat16)


def dot3(left, right, dims=((1,), (0,))):
    dims = (dims, ((), ()))
    dot = functools.partial(
        lax.dot_general, dimension_numbers=dims, preferred_element_type=jnp.float32
    )
    return dot(left[0], right[0]) + (dot(left[0], right[1]) + dot(left[1], right[0]))


def folded(wave):
    return jnp.where(wave > G // 2, wave - G, wave).astype(jnp.float32)


def slope(wave):
    w = wave.astype(jnp.float32)
    return (8.0 * sincos(w)[1] - sincos(2.0 * w)[1]) * (1.0 / 6.0)


def leaf_weights(u):
    members = u.shape[1]
    row = iota((PATCH, members), 0)
    cells = (row // PATCH_YZ, row // PZ % PY, row % PZ)
    product = None
    for c, extent in enumerate((PX, PY, PZ)):
        centre = cells[c].astype(jnp.float32) + 0.5
        coordinate = 0.5 + u[c : c + 1] * (extent - 1.0)
        w = jnp.maximum(0.0, 1.0 - jnp.abs(coordinate - centre))
        product = w if product is None else product * w
    return product


def pack(leaf_cell, tile_lists, fraction, masses, packed, book):
    leaves = packed.shape[0]
    members = masses.shape[1] // leaves
    lane = iota((1, members), 1)
    for n in range(leaves):
        at = slice(n * members, (n + 1) * members)
        u = fraction[:, at]
        m = masses[:, at]
        w = leaf_weights(u)
        full = jnp.broadcast_to(m, (8, members))
        packed[n : n + 1, 0:PATCH] = dot3(split(full), split(w), ((1,), (1,)))[0:1, :]
        cell = [leaf_cell[c, n].astype(jnp.float32) for c in range(3)]
        note = jnp.zeros((1, members), jnp.float32)
        for c in range(3):
            note = jnp.where(lane == c, cell[c], note)
        packed[n : n + 1, PATCH:] = note[:, 0:PATCH]
        for k in range(2):
            note = jnp.where(lane == 3 + k, tile_lists[k, n].astype(jnp.float32), note)
        for c, extent in enumerate((PX, PY, PZ)):
            book[n, c : c + 1, :] = cell[c] + (u[c : c + 1] * (extent - 1.0) + 0.5)
        book[n, 3:4, :] = m
        book[n, 4:5, :] = note
        book[n, 5:8, :] = jnp.zeros((3, members), jnp.float32)


def peers_of(axis):
    count = lax.axis_size(axis)
    me = lax.axis_index(axis)
    return [(axis, s, lax.rem(me + s, count), lax.rem(me + count - s, count)) for s in range(1, count)]


def greet(groups, meanwhile=None):
    barrier = pltpu.get_barrier_semaphore()
    for axis, _, ahead, _ in groups:
        pl.semaphore_signal(
            barrier, inc=1, device_id={axis: ahead}, device_id_type=pl.DeviceIdType.MESH
        )
    if meanwhile is not None:
        meanwhile()
    pl.semaphore_wait(barrier, len(groups))


def remote(src, dst, send, recv, axis, to):
    return pltpu.make_async_remote_copy(
        src_ref=src,
        dst_ref=dst,
        send_sem=send,
        recv_sem=recv,
        device_id={axis: to},
        device_id_type=pl.DeviceIdType.MESH,
    )


def gather_kernel(
    leaf_cell, tile_lists, fraction, masses, out, books, packed, book, own, sends, recvs
):
    wide, narrow = peers_of("wide"), peers_of("narrow")
    w, v = lax.axis_index("wide"), lax.axis_index("narrow")
    keep = [
        pltpu.make_async_copy(packed, out.at[w, v], own.at[0]),
        pltpu.make_async_copy(book, books.at[0], own.at[1]),
    ]

    def fill():
        pack(leaf_cell, tile_lists, fraction, masses, packed, book)
        for copy in keep:
            copy.start()
        for copy in keep:
            copy.wait()

    greet(wide + narrow, fill)
    at = 0
    first = []
    for axis, s, ahead, _ in narrow:
        first.append(remote(out.at[w, v], out.at[w, v], sends.at[at], recvs.at[at], axis, ahead))
        at += 1
    for copy in first:
        copy.start()
    near = []
    for slot, (axis, to) in enumerate(
        (
            ("wide", wide[-1][2]),
            ("wide", wide[0][2]),
            ("narrow", narrow[-1][2]),
            ("narrow", narrow[0][2]),
        )
    ):
        near.append(remote(books.at[0], books.at[slot + 1], sends.at[at], recvs.at[at], axis, to))
        at += 1
    for copy in near:
        copy.start()
    for copy, (axis, s, _, behind) in zip(first, narrow):
        remote(
            out.at[w, v], out.at[w, behind], sends.at[s - 1], recvs.at[s - 1], axis, behind
        ).wait_recv()
    second = []
    base = at
    for axis, s, ahead, _ in wide:
        second.append(remote(out.at[w], out.at[w], sends.at[at], recvs.at[at], axis, ahead))
        at += 1
    for copy in second:
        copy.start()
    for axis, s, _, behind in wide:
        i = base + s - 1
        remote(out.at[w], out.at[behind], sends.at[i], recvs.at[i], axis, behind).wait_recv()
    for copy in near:
        copy.wait_recv()
    for copy in first + second + near:
        copy.wait_send()


def modes_at(index, ny, origin):
    return origin[1] + index % ny, origin[0] + index // ny


def x_basis(x, lane):
    half = G // 2
    wave = jnp.where(lane > half, lane - half, lane).astype(jnp.float32)
    turn = jnp.where(lane > half, float(G // 4), 0.0)
    return sincos(x * wave - turn)[0]


def forward_tables(patches, e_hi, e_lo, p_cat):
    size = patches.shape[0]
    x_col = patches[:, PATCH : PATCH + 1]
    lane = iota((size, G), 1)
    group = iota((size, 4 * PATCH_YZ), 1) // PATCH_YZ
    for a in range(PX):
        at = slice(a * size, (a + 1) * size)
        e_hi[at, :], e_lo[at, :] = split(x_basis(x_col + float(a), lane))
        p = jnp.concatenate([patches[:, a * PATCH_YZ : (a + 1) * PATCH_YZ]] * 4, axis=1)
        hi = p.astype(jnp.bfloat16).astype(jnp.float32)
        p_cat[at, :] = jnp.where(
            group == 3, 0.0, jnp.where(group == 1, p - hi, hi)
        ).astype(jnp.bfloat16)


def inverse_tables(cells, e_hi, e_lo):
    size = cells.shape[1]
    row = iota((G, size), 0)
    for a in range(PX):
        at = slice(a * size, (a + 1) * size)
        e_hi[:, at], e_lo[:, at] = split(x_basis(cells[0:1, :] + float(a), row))


def phases(base, chunk, ny, origin, cells):
    ky, kz = modes_at(base + iota((chunk, 1), 0), ny, origin)
    return sincos(ky.astype(jnp.float32) * cells[1:2, :] + kz.astype(jnp.float32) * cells[2:3, :])


def forward_chunk(base, chunk, ny, origin, phase, e, p_cat):
    ky, kz = modes_at(base + iota((chunk, 1), 0), ny, origin)
    lane = iota((1, 4 * PATCH_YZ), 1)
    cell = lane % PATCH_YZ
    group = lane // PATCH_YZ
    tables = jnp.concatenate(
        sincos(
            ky.astype(jnp.float32) * (cell // PZ).astype(jnp.float32)
            + kz.astype(jnp.float32) * (cell % PZ).astype(jnp.float32)
        ),
        axis=0,
    )
    hi = tables.astype(jnp.bfloat16).astype(jnp.float32)
    tables = jnp.where(group == 3, 0.0, jnp.where(group == 2, tables - hi, hi))
    f = lax.dot_general(
        tables.astype(jnp.bfloat16),
        p_cat,
        (((1,), (1,)), ((), ())),
        preferred_element_type=jnp.float32,
    )
    fc, fs = f[:chunk], f[chunk:]
    c, s = (jnp.concatenate([part] * PX, axis=1) for part in phase)
    m = jnp.concatenate([fc * c - fs * s, -(fc * s + fs * c)], axis=0)
    return dot3(split(m), e)


def apply_green(base, chunk, ny, origin, q):
    ky, kz = modes_at(base + iota((chunk, 1), 0), ny, origin)
    half = G // 2
    lane = iota((1, G), 1)
    unit = 2.0 * math.pi / G
    fx = jnp.where(lane > half, lane - half, lane).astype(jnp.float32) * unit
    fy, fz = folded(ky) * unit, folded(kz) * unit
    total = fx * fx + (fy * fy + fz * fz)
    divisor = jnp.where(total > 0, total, 1.0)
    green = jnp.where(
        total > 0, -4.0 * math.pi * jnp.exp(-total * (SCREEN * SCREEN)) / divisor, 0.0
    )
    green = green * jnp.where(lane % half == 0, 1.0, 2.0)
    return q * jnp.concatenate([green, green], axis=0)


def inverse_chunk(base, chunk, ny, origin, phase, e, h, acc):
    half = G // 2
    dx = slope(iota((1, half), 1))
    hx = jnp.concatenate([-(h[:, half:] * dx), h[:, :half] * dx], axis=1)
    lane = iota((1, 2 * chunk), 1)
    ky, kz = modes_at(base + lane % chunk, ny, origin)
    row = iota((PATCH_YZ, 1), 0)
    turn = jnp.where(lane < chunk, float(G // 4), 0.0)
    weight = jnp.where(
        (kz == 0) | (kz == half), 1.0, jnp.where(kz < half, 2.0, 0.0)
    ) * (1.0 / float(G * G * G))
    angle = ky.astype(jnp.float32) * (row // PZ).astype(jnp.float32) + kz.astype(jnp.float32) * (
        row % PZ
    ).astype(jnp.float32)
    slopes = sincos(angle - turn)[0] * weight
    c, s = (jnp.concatenate([part] * PX, axis=1) for part in phase)

    def add(source, at, table):
        p = dot3(split(source), e)
        real, imag = p[:chunk], p[chunk:]
        turned = split(jnp.concatenate([real * c - imag * s, real * s + imag * c], axis=0))
        hi, lo = split(table)
        rows = table.shape[0]
        dot = functools.partial(jnp.dot, preferred_element_type=jnp.float32)
        both = dot(jnp.concatenate([hi, lo], axis=0), turned[0])
        acc[at, :] += both[:rows] + (both[rows:] + dot(hi, turned[1]))

    cosine = sincos(angle - turn + float(G // 4))[0] * weight
    add(hx, slice(0, PATCH_YZ), cosine)
    add(
        h,
        slice(PATCH_YZ, 3 * PATCH_YZ),
        jnp.concatenate([slopes * slope(ky), slopes * slope(kz)], axis=0),
    )


def write_field(acc, out):
    size = out.shape[0]
    for f in range(3):
        for a in range(PX):
            block = acc[f * PATCH_YZ : (f + 1) * PATCH_YZ, a * size : (a + 1) * size]
            col = f * PATCH + a * PATCH_YZ
            out[:, col : col + PATCH_YZ] = block.T


def whole_kernel(ny, chunk, modes, origin, patches, out, e_hi, e_lo, p_cat, i_hi, i_lo, acc):
    cells = patches[:, PATCH:].T
    forward_tables(patches, e_hi, e_lo, p_cat)
    inverse_tables(cells, i_hi, i_lo)
    acc[...] = jnp.zeros_like(acc)

    def body(i, carry):
        base = i * chunk
        phase = phases(base, chunk, ny, origin, cells)
        q = forward_chunk(base, chunk, ny, origin, phase, (e_hi[...], e_lo[...]), p_cat[...])
        h = apply_green(base, chunk, ny, origin, q)
        inverse_chunk(base, chunk, ny, origin, phase, (i_hi[...], i_lo[...]), h, acc)
        return carry

    lax.fori_loop(0, modes // chunk, body, 0)
    write_field(acc, out)


def forward_kernel(ny, chunk, origin, patches, out, e_hi, e_lo, p_cat):
    step = pl.program_id(0)
    cells = patches[:, PATCH:].T
    forward_tables(patches, e_hi, e_lo, p_cat)

    @pl.when(step == 0)
    def _():
        out[...] = jnp.zeros_like(out)

    def body(i, carry):
        base = i * chunk
        at = pl.ds(pl.multiple_of(2 * base, 8), 2 * chunk)
        phase = phases(base, chunk, ny, origin, cells)
        out[at, :] += forward_chunk(
            base, chunk, ny, origin, phase, (e_hi[...], e_lo[...]), p_cat[...]
        )

        @pl.when(step == pl.num_programs(0) - 1)
        def _():
            out[at, :] = apply_green(base, chunk, ny, origin, out[at, :])

        return carry

    lax.fori_loop(0, out.shape[0] // (2 * chunk), body, 0)


def inverse_kernel(ny, chunk, origin, spectrum, patches, out, i_hi, i_lo, acc):
    cells = patches[:, PATCH:].T
    inverse_tables(cells, i_hi, i_lo)
    acc[...] = jnp.zeros_like(acc)

    def body(i, carry):
        base = i * chunk
        at = pl.ds(pl.multiple_of(2 * base, 8), 2 * chunk)
        phase = phases(base, chunk, ny, origin, cells)
        inverse_chunk(
            base, chunk, ny, origin, phase, (i_hi[...], i_lo[...]), spectrum[at, :], acc
        )
        return carry

    lax.fori_loop(0, spectrum.shape[0] // (2 * chunk), body, 0)
    write_field(acc, out)


def pair_jobs(leaves, slots, exports, notes, books, forces):
    def job(j, rank, target):
        tgt = books[0, target]
        total = [0.0, 0.0, 0.0]
        for k in range(2):
            source = notes[rank, target, 3 + k]
            src = books[rank, source]
            cols = src.T
            members = src.shape[1]
            d = []
            for c in range(3):
                apart = (notes[rank, source, c] - notes[0, target, c]).astype(jnp.float32)
                wraps = (apart > 0.5 * G).astype(jnp.int32) - (apart <= -0.5 * G).astype(jnp.int32)
                col = cols[:, c : c + 1] - float(G) * wraps.astype(jnp.float32)
                d.append(jnp.broadcast_to(col, (members, members)) - tgt[c : c + 1, :])
            squared = d[0] * d[0] + d[1] * d[1] + d[2] * d[2]
            r = squared * lax.rsqrt(jnp.maximum(squared, 1e-30))
            t = 1.0 / (1.0 + 0.5 * r)
            poly = ERFCX[-1] * t + ERFCX[-2]
            for coefficient in ERFCX[-3::-1]:
                poly = poly * t + coefficient
            screened = jnp.exp(-squared) * (poly * t + (2.0 / math.sqrt(math.pi)) * r)
            inv = lax.rsqrt(squared + SOFTEN * SOFTEN)
            w = cols[:, 3:4] * screened * (inv * inv * inv)
            for c in range(3):
                total[c] = total[c] + jnp.sum(w * d[c], axis=0, keepdims=True)
        forces[j] = jnp.concatenate(total + [jnp.zeros((5,) + total[0].shape[1:], jnp.float32)], axis=0)

    def own(n, carry):
        job(n, 0, n)
        return carry

    def guest(j, carry):
        face = j // slots
        job(leaves + j, face + 1, jnp.minimum(exports[face, j % slots], leaves - 1))
        return carry

    lax.fori_loop(0, leaves, own, 0)
    lax.fori_loop(0, 4 * slots, guest, 0)


def finish_kernel(
    exports, notes, books, fraction, partial, out, landed, mine, near, forces, w_hi, w_lo, sends, recvs
):
    wide, narrow = peers_of("wide"), peers_of("narrow")
    w, v = lax.axis_index("wide"), lax.axis_index("narrow")
    leaves = mine.shape[1]
    slots = exports.shape[1]
    members = fraction.shape[1] // leaves
    greet(wide + narrow)
    at = 0
    first = []
    for axis, s, ahead, _ in wide:
        first.append(
            remote(partial.at[ahead], landed.at[s - 1], sends.at[at], recvs.at[at], axis, ahead)
        )
        at += 1
    for copy in first:
        copy.start()
    pair_jobs(leaves, slots, exports, notes, books, forces)
    for copy in first:
        copy.wait_recv()
    total = partial[w]
    for s in range(len(wide)):
        total = total + landed[s]
    mine[...] = total
    second = []
    for axis, s, ahead, _ in narrow:
        second.append(
            remote(mine.at[ahead], near.at[s - 1], sends.at[at], recvs.at[at], axis, ahead)
        )
        at += 1
    for copy in second:
        copy.start()
    short = []
    for n in range(leaves):
        w_hi[n], w_lo[n] = split(leaf_weights(fraction[:, n * members : (n + 1) * members]))
        force = forces[n]
        for j in range(4 * slots):
            mine_too = jnp.where(exports[j // slots, j % slots] == n, 1.0, 0.0)
            force = force + forces[leaves + j] * mine_too
        short.append(force)
    for copy in second:
        copy.wait_recv()
    field = mine[v]
    for s in range(len(narrow)):
        field = field + near[s]
    for n in range(leaves):
        values = jnp.concatenate(
            [field[n : n + 1, f * PATCH : (f + 1) * PATCH] for f in range(3)], axis=0
        )
        got = dot3(split(values), (w_hi[n], w_lo[n]))
        out[:, n * members : (n + 1) * members] = got + short[n][0:3, :]
    for copy in first + second:
        copy.wait_send()


def local(fraction, masses, leaf_cell, exports, tile_lists):
    leaves = leaf_cell.shape[1]
    members = masses.shape[0] // leaves
    slots = exports.shape[1]
    n_wide, n_narrow = lax.axis_size("wide"), lax.axis_size("narrow")
    total = leaves * n_wide * n_narrow
    f32 = jnp.float32

    copies = n_wide - 1 + n_narrow - 1
    gathered, books = pl.pallas_call(
        gather_kernel,
        out_shape=(
            jax.ShapeDtypeStruct((n_wide, n_narrow, leaves, 2 * PATCH), f32),
            jax.ShapeDtypeStruct((5, leaves, 8, members), f32),
        ),
        in_specs=[SMEM, SMEM, VMEM, VMEM],
        out_specs=(VMEM, VMEM),
        scratch_shapes=[
            pltpu.VMEM((leaves, 2 * PATCH), f32),
            pltpu.VMEM((leaves, 8, members), f32),
            pltpu.SemaphoreType.DMA((2,)),
            pltpu.SemaphoreType.DMA((copies + 4,)),
            pltpu.SemaphoreType.DMA((copies + 4,)),
        ],
        compiler_params=pltpu.CompilerParams(collective_id=0, has_side_effects=True),
        name="gather",
    )(leaf_cell, tile_lists, fraction, masses.reshape(1, -1))
    gathered = gathered.reshape(total, 2 * PATCH)
    notes = books[:, :, 4, 0:5].astype(jnp.int32)
    nz = -(-(G // 2 + 1) // n_narrow)
    ny = G // n_wide
    modes = nz * ny
    parts = next(p for p in range(1, modes + 1) if nz % p == 0 and modes // p <= 384)
    chunk = modes // parts
    origin = jnp.stack([lax.axis_index("narrow") * nz, lax.axis_index("wide") * ny]).astype(
        jnp.int32
    )
    size = min(total, 256)
    blocks = total // size
    params = pltpu.CompilerParams(vmem_limit_bytes=56 * 2**20)
    forward_scratch = [
        pltpu.VMEM((PX * size, G), jnp.bfloat16),
        pltpu.VMEM((PX * size, G), jnp.bfloat16),
        pltpu.VMEM((PX * size, 4 * PATCH_YZ), jnp.bfloat16),
    ]
    inverse_scratch = [
        pltpu.VMEM((G, PX * size), jnp.bfloat16),
        pltpu.VMEM((G, PX * size), jnp.bfloat16),
        pltpu.VMEM((3 * PATCH_YZ, PX * size), f32),
    ]
    field_shape = jax.ShapeDtypeStruct((total, 3 * PATCH), f32)
    leaf_rows = pl.BlockSpec((size, 2 * PATCH), lambda i: (i, 0))
    spectrum_all = pl.BlockSpec((2 * modes, G), lambda i: (0, 0))
    if blocks == 1:
        partial = pl.pallas_call(
            functools.partial(whole_kernel, ny, chunk, modes),
            out_shape=field_shape,
            in_specs=[SMEM, VMEM],
            out_specs=VMEM,
            scratch_shapes=forward_scratch + inverse_scratch,
            compiler_params=params,
            name="transform",
        )(origin, gathered)
    else:
        spectrum = pl.pallas_call(
            functools.partial(forward_kernel, ny, chunk),
            grid=(blocks,),
            out_shape=jax.ShapeDtypeStruct((2 * modes, G), f32),
            in_specs=[SMEM, leaf_rows],
            out_specs=spectrum_all,
            scratch_shapes=forward_scratch,
            compiler_params=params,
            name="forward",
        )(origin, gathered)
        partial = pl.pallas_call(
            functools.partial(inverse_kernel, ny, chunk),
            grid=(blocks,),
            out_shape=field_shape,
            in_specs=[SMEM, spectrum_all, leaf_rows],
            out_specs=pl.BlockSpec((size, 3 * PATCH), lambda i: (i, 0)),
            scratch_shapes=inverse_scratch,
            compiler_params=params,
            name="inverse",
        )(origin, spectrum, gathered)
    block = (leaves, 3 * PATCH)
    return pl.pallas_call(
        finish_kernel,
        out_shape=jax.ShapeDtypeStruct((3, leaves * members), f32),
        in_specs=[SMEM, SMEM, VMEM, VMEM, VMEM],
        out_specs=VMEM,
        scratch_shapes=[
            pltpu.VMEM((n_wide - 1, n_narrow) + block, f32),
            pltpu.VMEM((n_narrow,) + block, f32),
            pltpu.VMEM((n_narrow - 1,) + block, f32),
            pltpu.VMEM((leaves + 4 * slots, 8, members), f32),
            pltpu.VMEM((leaves, PATCH, members), jnp.bfloat16),
            pltpu.VMEM((leaves, PATCH, members), jnp.bfloat16),
            pltpu.SemaphoreType.DMA((copies,)),
            pltpu.SemaphoreType.DMA((copies,)),
        ],
        compiler_params=pltpu.CompilerParams(collective_id=1, has_side_effects=True),
        name="finish",
    )(exports, notes, books, fraction, partial.reshape((n_wide, n_narrow) + block))


def solution(mesh):
    placed = (
        P(None, ("wide", "narrow")),
        P(("wide", "narrow")),
        P(None, ("wide", "narrow")),
        P(None, ("wide", "narrow")),
        P(None, ("wide", "narrow")),
    )
    return jax.shard_map(
        local, mesh=mesh, in_specs=placed, out_specs=P(None, ("wide", "narrow")), check_vma=False
    )
```
